256 devices in a mesh: rep: 8 (over z_lo, core), dp: 32 (over z_hi, x, y).
Axes of the slice: x: 4, y: 4, z: 8 (z_hi: 2, z_lo: 4; z = z_hi * 4 + z_lo), core: 2. Of those that a mesh axis runs over, the one named last changes fastest.
Arguments:
- hidden: bfloat16 [2, 8, 16384, 1920], P(None, 'rep', 'dp'), may hold values from -6 to 6
- partners: int32 [2, 8], replicated, may hold values from 0 to 7, as said below
- frame_mask: int32 [2, 16384], P(None, 'dp'), may hold values 0 or 1
- segment_ids: int32 [2, 16384], P(None, 'dp'), may hold values from 0 to 7, as said below
- master: float32 [8, 1920, 500], P('rep', 'dp'), may hold values from -0.125 to 0.125
- moment_one: float32 [8, 1920, 500], P('rep', 'dp'), may hold values from -3 to 3
- moment_two: float32 [8, 1920, 500], P('rep', 'dp'), may hold values from 0.1 to 10
Outputs:
- hidden_grad: bfloat16 [2, 8, 16384, 1920], P(None, 'rep', 'dp')
- new_master: float32 [8, 1920, 500], P('rep', 'dp')
- new_moment_one: float32 [8, 1920, 500], P('rep', 'dp')
- new_moment_two: float32 [8, 1920, 500], P('rep', 'dp')
The draws below stay inside these ranges and needn't reach their ends.
Inputs may be any that keep to these rules, and one draw needn't show every extreme that they name: `partners`: each row is a permutation of the replicas forming one cycle through all of them, so no replica is its own partner. `segment_ids`: within each aligned block of 512 frames the ids start at 0 and never fall.
All inputs are finite; a program needn't handle non-finite values. No bound on the sum of `frame_mask` on one device may be relied on, other than what follows from the above.
Results may differ from the reference program's by a relative error of at most 0.035.
Values may be sent and summed in bfloat16 or wider, within the bound.
A program may use at most 64 MiB of HBM per device.

```python
import math
import jax
import jax.numpy as jnp
from jax import lax

D = 1920
V = 500
SEGS = 8
TOK_DEV = 512
REPLICAS = 8
TOKENS = 16384


def draw_partners(key, part):
    result = []
    for micro in range(2):
        order = jax.random.permutation(jax.random.fold_in(key, 11 + micro), REPLICAS).astype(jnp.int32)
        following = jnp.roll(order, -1)
        result.append(jnp.zeros((REPLICAS,), jnp.int32).at[order].set(following))
    return jnp.stack(result)


def draw_segment_ids(key, part):
    blocks = TOKENS // TOK_DEV
    draws = jax.random.randint(jax.random.fold_in(key, 29), (2, blocks, TOK_DEV), 0, TOK_DEV)
    starts = (draws < SEGS - 1).astype(jnp.int32)
    starts = starts.at[:, :, 0].set(0)
    ids = jnp.minimum(jnp.cumsum(starts, axis=-1), SEGS - 1).astype(jnp.int32)
    return ids.reshape(2, TOKENS)


def set_ends(values, stream_key, least, high):
    place = [jax.random.randint(jax.random.fold_in(stream_key, axis), (), 0, length) for axis, length in enumerate(values.shape)]
    widest = values.shape.index(max(values.shape))
    beside = place[:widest] + [(place[widest] + 1) % values.shape[widest]] + place[widest + 1:]
    return values.at[tuple(place)].set(least).at[tuple(beside)].set(high)


def shard_levels(rng, dims, shards, least, largest):
    level, own = 1.0, jax.random.fold_in(rng, 6)
    for position, shards_of in shards:
        steps = jnp.exp(jax.random.uniform(jax.random.fold_in(own, position), (shards_of,), jnp.float32, least / len(shards), largest / len(shards)))
        level = level * jnp.repeat(steps, dims[position] // shards_of).reshape([-1 if axis == position else 1 for axis in range(len(dims))])
    return level


def bell_draw(own_key, dims, scale, bound, shards=(), held_as=jnp.bfloat16):
    loudness = shard_levels(own_key, dims, shards, -0.22, 0.18) if shards else 1.0
    values = jax.random.normal(own_key, dims, jnp.float32) * scale * loudness
    return jnp.minimum(jnp.maximum(values, -bound), bound).astype(held_as)


def setup_inputs(seed: int = 0) -> dict:
    key_list = jax.random.split(jax.random.key(seed), 8)
    return {
        "hidden": bell_draw(key_list[0], (2, REPLICAS, TOKENS, D), 1.0, 6.0, ((1, 8), (2, 32))),
        "partners": draw_partners(jax.random.fold_in(key_list[7], 71), 0),
        "frame_mask": set_ends((jax.random.randint(key_list[2], (2, TOKENS), 0, 4) < 3).astype(jnp.int32), jax.random.fold_in(key_list[2], 1), 0, 1),
        "segment_ids": draw_segment_ids(jax.random.fold_in(key_list[7], 71), 0),
        "master": bell_draw(key_list[4], (REPLICAS, D, V), D ** -0.5, 0.125, ((0, 8), (1, 32)), jnp.float32),
        "moment_one": bell_draw(key_list[5], (REPLICAS, D, V), 0.5, 3.0, ((0, 8), (1, 32)), jnp.float32),
        "moment_two": jnp.clip(jnp.exp(math.log(10.0) - 4.6051702 * jax.random.uniform(key_list[6], (REPLICAS, D, V), jnp.float32) ** shard_levels(key_list[6], (REPLICAS, D, V), ((0, 8), (1, 32)), -0.2, 0.2)), 0.1, 10.0),
    }


def frame_scale(frame_mask, segment_ids):
    blocks = TOKENS // TOK_DEV
    ids = segment_ids.reshape(2, blocks, TOK_DEV)
    valid = frame_mask.reshape(2, blocks, TOK_DEV).astype(jnp.float32)
    onehot = (ids[..., None] == jnp.arange(SEGS, dtype=jnp.int32)).astype(jnp.float32)
    counts = lax.optimization_barrier(jnp.sum(onehot * valid[..., None], axis=2))
    per_frame = lax.optimization_barrier(jnp.sum(onehot * counts[:, :, None, :], axis=-1))
    return (valid / jnp.maximum(per_frame, 1.0)).reshape(2, TOKENS)

def reference(hidden, partners, frame_mask, segment_ids, master, moment_one, moment_two):
    scale = frame_scale(frame_mask, segment_ids)
    head_low = master.astype(jnp.bfloat16)
    logits = jnp.stack([jnp.stack([jnp.dot(hidden[m, r], head_low[r], preferred_element_type=jnp.float32) for r in range(REPLICAS)]) for m in range(2)])
    sent = logits.astype(jnp.bfloat16)
    grads_out = []
    hidden_out = []
    for m in range(2):
        other = jnp.take(sent[m], partners[m].astype(jnp.int32), axis=0).astype(jnp.float32)
        grad = ((logits[m] - other) * scale[m][None, :, None]).astype(jnp.bfloat16)
        grads_out.append(grad)
        hidden_out.append(jnp.stack([jnp.dot(grad[r], head_low[r].T, preferred_element_type=jnp.float32).astype(jnp.bfloat16) for r in range(REPLICAS)]))
    hidden_grad = jnp.stack(hidden_out)
    head_grad = jnp.stack([jnp.dot(hidden[0, r].T, grads_out[0][r], preferred_element_type=jnp.float32) + jnp.dot(hidden[1, r].T, grads_out[1][r], preferred_element_type=jnp.float32) for r in range(REPLICAS)])
    new_moment_one = 0.9 * moment_one + 0.1 * head_grad
    new_moment_two = 0.99 * moment_two + 0.01 * head_grad * head_grad
    new_master = master - 0.01 * new_moment_one / (jnp.sqrt(new_moment_two) + 1e-08)
    return (hidden_grad, new_master, new_moment_one, new_moment_two)
```

```python
import functools

import jax
import jax.numpy as jnp
from jax import lax
from jax.experimental import pallas as pl
from jax.experimental.pallas import tpu as pltpu
from jax.sharding import Mesh
from jax.sharding import PartitionSpec as P

MESH = pl.DeviceIdType.MESH
F32 = jnp.float32
BF16 = jnp.bfloat16
SEGS = 8
REPS = 8
LANES = 128
CHUNK = 256
ROWS = 60
PAD = 64
GROUP = 4 * ROWS


def spread(transposed):
    shape = (4 * PAD, GROUP) if transposed else (GROUP, 4 * PAD)
    packed = lax.broadcasted_iota(jnp.int32, shape, 1 if transposed else 0)
    padded = lax.broadcasted_iota(jnp.int32, shape, 0 if transposed else 1)
    moved = packed
    for k in (1, 2, 3):
        moved = moved + jnp.where(packed >= k * ROWS, PAD - ROWS, 0)
    return jnp.where(moved == padded, 1.0, 0.0).astype(BF16)


def kernel(
    partners, mask, segs, master, mom1, mom2, hidden_hbm,
    hg_hbm, new_master, new_m1, new_m2,
    hid, hid_t, hp, head, logits, sent, got_0, got_1, got_2, got_3, stage, other, scale, grad, hg,
    dw, r1, s2, r2, s3, r3,
    local_sem, out_sem, z_s, z_r, a_s, a_r, b_s, b_r, p1_s, p1_r, p2_s, p2_r,
    c_s, c_r, d_s, d_r, e_s, e_r,
):
    zl, co = lax.axis_index("zl"), lax.axis_index("co")
    zh, x, y = lax.axis_index("zh"), lax.axis_index("x"), lax.axis_index("y")
    me = zl * 2 + co
    tokens = hid.shape[0] // 2
    part = tokens // REPS
    got = (got_0, got_1, got_2, got_3)

    load = pltpu.make_async_copy(hidden_hbm, hid, local_sem)
    load.start()

    def rep_of(d):
        to = lax.rem(me + d, REPS)
        return to, {"zl": to // 2, "co": lax.rem(to, 2)}

    def on(axis, d):
        if axis == "zh":
            to = 1 - zh
        else:
            to = lax.rem((x if axis == "x" else y) + d, 4)
        return to, {axis: to}

    barrier = pltpu.get_barrier_semaphore()
    peers = [on("zh", 1)[1]] + [on(a, d)[1] for a in ("x", "y") for d in (1, 2, 3)]
    peers += [rep_of(d)[1] for d in range(1, REPS)]
    for peer in peers:
        pl.semaphore_signal(barrier, inc=1, device_id=peer, device_id_type=MESH)

    low = master[...].astype(BF16)
    vocab = low.shape[1]
    for s in range(4):
        cols = min(LANES, vocab - s * LANES)
        piece = low[:, s * LANES : s * LANES + cols]
        if cols < LANES:
            piece = jnp.concatenate([piece, jnp.zeros((ROWS, LANES - cols), BF16)], axis=1)
        piece = jnp.concatenate([piece, jnp.zeros((PAD - ROWS, LANES), BF16)], axis=0)
        hp[s, zh, x, y] = piece

    pl.semaphore_wait(barrier, len(peers))

    def send(src, dst, send_sem, recv_sem, peer):
        copy = pltpu.make_async_remote_copy(
            src_ref=src, dst_ref=dst, send_sem=send_sem, recv_sem=recv_sem,
            device_id=peer, device_id_type=MESH,
        )
        copy.start()
        return copy

    started = []

    z_copies, a_copies, b_copies = {}, {}, {}
    for s in range(4):
        ref = hp.at[s, zh, x, y]
        z_copies[s] = send(ref, ref, z_s.at[s], z_r.at[s], on("zh", 1)[1])
    for s in range(4):
        z_copies[s].wait_recv()
        ref = hp.at[s, :, x, y]
        first = "x" if s % 2 == 0 else "y"
        a_copies[s] = [
            send(ref, ref, a_s.at[s, d - 1], a_r.at[s, d - 1], on(first, d)[1]) for d in (1, 2, 3)
        ]
    for s in range(4):
        for copy in a_copies[s]:
            copy.wait_recv()
        if s % 2 == 0:
            ref, second = hp.at[s, :, :, y], "y"
        else:
            ref, second = hp.at[s, :, x], "x"
        b_copies[s] = [
            send(ref, ref, b_s.at[s, d - 1], b_r.at[s, d - 1], on(second, d)[1]) for d in (1, 2, 3)
        ]

    for m in range(2):
        valid = mask[m : m + 1, :].astype(F32)
        ids = segs[m : m + 1, :]
        onehot = (lax.broadcasted_iota(jnp.int32, (SEGS, tokens), 0) == ids).astype(F32)
        counts = jnp.sum(onehot * valid, axis=1, keepdims=True)
        per_frame = jnp.sum(onehot * counts, axis=0, keepdims=True)
        row = valid / jnp.maximum(per_frame, 1.0)
        wide = jnp.broadcast_to(row, (LANES, tokens))
        scale[m * tokens : (m + 1) * tokens, :] = wide.T

    load.wait()

    @pl.loop(0, hid.shape[1] // LANES)
    def _(j):
        at = pl.ds(pl.multiple_of(j * LANES, LANES), LANES)
        hid_t[at, :] = hid[:, at].T

    pack = spread(False)
    p1, p2 = {}, {}
    for c in range(2):
        lanes = slice(c * CHUNK, (c + 1) * CHUNK)
        for s in (2 * c, 2 * c + 1):
            for copy in b_copies[s]:
                copy.wait_recv()

        @pl.loop(0, 8)
        def _(g):
            rows = pl.ds(pl.multiple_of(g * GROUP, 16), GROUP)
            for s in (2 * c, 2 * c + 1):
                block = hp[s, g // 4, lax.rem(g, 4)].reshape(4 * PAD, LANES)
                head[rows, s * LANES : (s + 1) * LANES] = jnp.dot(
                    pack, block, preferred_element_type=F32
                ).astype(BF16)

        for m in range(2):

            @pl.loop(0, 2)
            def _(t):
                rows = pl.ds(pl.multiple_of(m * tokens + t * 4 * part, 4 * part), 4 * part)
                block = jnp.dot(hid[rows, :], head[:, lanes], preferred_element_type=F32)
                block = block.reshape(4, part, CHUNK)
                logits[m, pl.ds(t * 4, 4), :, lanes] = block
                sent[m, pl.ds(t * 4, 4), :, lanes] = block.astype(BF16)

            u = 2 * c + m
            p1[u] = []
            for d in range(1, REPS):
                to, peer = rep_of(d)
                p1[u].append(
                    send(sent.at[m, to, :, lanes], got[u].at[me], p1_s.at[u, d - 1], p1_r.at[u, d - 1], peer)
                )
            got[u][me] = sent[m, me, :, lanes]

    for u in range(4):
        c, m = u // 2, u % 2
        lanes = slice(c * CHUNK, (c + 1) * CHUNK)
        for copy in p1[u]:
            copy.wait_recv()
        p2[u] = []
        for d in range(1, REPS):
            to, peer = rep_of(d)
            stage[u, d - 1] = got[u][partners[m, to]]
            p2[u].append(
                send(stage.at[u, d - 1], other.at[m, me, :, lanes], p2_s.at[u, d - 1], p2_r.at[u, d - 1], peer)
            )
        other[m, me, :, lanes] = got[u][partners[m, me]]

    grow = spread(True)

    def gradient(c):
        lanes = slice(c * CHUNK, (c + 1) * CHUNK)
        for m in range(2):
            for copy in p2[2 * c + m]:
                copy.wait_recv()

            @pl.loop(0, REPS)
            def _(k):
                rows = pl.ds(pl.multiple_of((m * REPS + k) * part, part), part)
                by = scale[rows, :]
                for s in (2 * c, 2 * c + 1):
                    at = slice(s * LANES, (s + 1) * LANES)
                    diff = logits[m, k, :, at] - other[m, k, :, at].astype(F32)
                    grad[rows, at] = (diff * by).astype(BF16)

        @pl.loop(0, 8)
        def _(g):
            rows = pl.ds(pl.multiple_of(g * GROUP, 16), GROUP)
            block = jnp.dot(hid_t[rows, :], grad[:, lanes], preferred_element_type=F32).astype(BF16)
            block = jnp.dot(grow, block, preferred_element_type=F32).astype(BF16)
            for s in range(2):
                dw[2 * c + s, g // 4, lax.rem(g, 4)] = block[:, s * LANES : (s + 1) * LANES].reshape(4, PAD, LANES)

        copies = {}
        for s in (2 * c, 2 * c + 1):
            copies[s] = []
            for d in (1, 2, 3):
                to, peer = on("y" if s % 2 == 0 else "x", d)
                src = dw.at[s, :, :, to] if s % 2 == 0 else dw.at[s, :, to]
                copies[s].append(send(src, r1.at[s, d - 1], c_s.at[s, d - 1], c_r.at[s, d - 1], peer))
        return copies

    def second(c, copies):
        after = {}
        for s in (2 * c, 2 * c + 1):
            for copy in copies[s]:
                copy.wait_recv()

            @pl.loop(0, 8)
            def _(g):
                i, k = g // 4, lax.rem(g, 4)
                own = dw[s, i, k, y] if s % 2 == 0 else dw[s, i, x, k]
                total = own.astype(F32)
                for d in range(3):
                    total = total + r1[s, d, i, k].astype(F32)
                s2[s, i, k] = total.astype(BF16)

            after[s] = []
            for d in (1, 2, 3):
                to, peer = on("x" if s % 2 == 0 else "y", d)
                after[s].append(
                    send(s2.at[s, :, to], r2.at[s, d - 1], d_s.at[s, d - 1], d_r.at[s, d - 1], peer)
                )
        return after

    def third(c, copies):
        last = {}
        for s in (2 * c, 2 * c + 1):
            for copy in copies[s]:
                copy.wait_recv()
            mine = x if s % 2 == 0 else y
            for i in range(2):
                total = s2[s, i, mine].astype(F32)
                for d in range(3):
                    total = total + r2[s, d, i].astype(F32)
                s3[s, i] = total.astype(BF16)
            last[s] = send(s3.at[s, 1 - zh], r3.at[s], e_s.at[s], e_r.at[s], on("zh", 1)[1])
        return last

    def adam(c, copies):
        for s in (2 * c, 2 * c + 1):
            copies[s].wait_recv()
            cols = min(LANES, vocab - s * LANES)
            at = slice(s * LANES, s * LANES + cols)
            total = s3[s, zh].astype(F32) + r3[s].astype(F32)
            g = total[:ROWS, :cols]
            one = 0.9 * mom1[:, at] + 0.1 * g
            two = 0.99 * mom2[:, at] + 0.01 * g * g
            new_m1[:, at] = one
            new_m2[:, at] = two
            new_master[:, at] = master[:, at] - 0.01 * one / (jnp.sqrt(two) + 1e-08)

    first_0 = gradient(0)
    second_0 = second(0, first_0)
    first_1 = gradient(1)
    third_0 = third(0, second_0)

    outs = []
    width = hid.shape[1] // 5
    height = hid.shape[0] // 4
    for t in range(4):
        rows = slice(t * height, (t + 1) * height)

        @pl.loop(0, 5)
        def _(n):
            at = pl.ds(pl.multiple_of(n * width, LANES), width)
            block = lax.dot_general(
                grad[rows, :], head[at, :], (((1,), (1,)), ((), ())), preferred_element_type=F32
            )
            hg[rows, at] = block.astype(BF16)

        out = pltpu.make_async_copy(hg.at[rows], hg_hbm.at[rows], out_sem.at[t])
        out.start()
        outs.append(out)
        if t == 1:
            second_1 = second(1, first_1)

    third_1 = third(1, second_1)
    adam(0, third_0)
    adam(1, third_1)

    for out in outs:
        out.wait()
    for group in (z_copies, third_0, third_1):
        started += list(group.values())
    for group in (a_copies, b_copies, p1, p2, first_0, first_1, second_0, second_1):
        for copies in group.values():
            started += copies
    for copy in started:
        copy.wait_send()


def per_device(hidden, partners, frame_mask, segment_ids, master, moment_one, moment_two):
    tokens, depth = hidden.shape[2:]
    frames = 2 * tokens
    part = tokens // REPS
    width = 4 * LANES
    vocab = master.shape[2]
    vmem = pl.BlockSpec(memory_space=pltpu.VMEM)
    hbm = pl.BlockSpec(memory_space=pl.ANY)
    small = jax.ShapeDtypeStruct((ROWS, vocab), F32)
    dma = pltpu.SemaphoreType.DMA
    hg, new_master, m1, m2 = pl.pallas_call(
        kernel,
        out_shape=(jax.ShapeDtypeStruct((frames, depth), BF16), small, small, small),
        in_specs=[pl.BlockSpec(memory_space=pltpu.SMEM)] + [vmem] * 5 + [hbm],
        out_specs=(hbm, vmem, vmem, vmem),
        scratch_shapes=[
            pltpu.VMEM((frames, depth), BF16),
            pltpu.VMEM((depth, frames), BF16),
            pltpu.VMEM((4, 2, 4, 4, PAD, LANES), BF16),
            pltpu.VMEM((depth, width), BF16),
            pltpu.VMEM((2, REPS, part, width), F32),
            pltpu.VMEM((2, REPS, part, width), BF16),
            pltpu.VMEM((REPS, part, CHUNK), BF16),
            pltpu.VMEM((REPS, part, CHUNK), BF16),
            pltpu.VMEM((REPS, part, CHUNK), BF16),
            pltpu.VMEM((REPS, part, CHUNK), BF16),
            pltpu.VMEM((4, REPS - 1, part, CHUNK), BF16),
            pltpu.VMEM((2, REPS, part, width), BF16),
            pltpu.VMEM((frames, LANES), F32),
            pltpu.VMEM((frames, width), BF16),
            pltpu.VMEM((frames, depth), BF16),
            pltpu.VMEM((4, 2, 4, 4, PAD, LANES), BF16),
            pltpu.VMEM((4, 3, 2, 4, PAD, LANES), BF16),
            pltpu.VMEM((4, 2, 4, PAD, LANES), BF16),
            pltpu.VMEM((4, 3, 2, PAD, LANES), BF16),
            pltpu.VMEM((4, 2, PAD, LANES), BF16),
            pltpu.VMEM((4, PAD, LANES), BF16),
            dma, dma((4,)),
            dma((4,)), dma((4,)),
            dma((4, 3)), dma((4, 3)),
            dma((4, 3)), dma((4, 3)),
            dma((4, 7)), dma((4, 7)),
            dma((4, 7)), dma((4, 7)),
            dma((4, 3)), dma((4, 3)),
            dma((4, 3)), dma((4, 3)),
            dma((4,)), dma((4,)),
        ],
        compiler_params=pltpu.CompilerParams(
            collective_id=0, has_side_effects=True, vmem_limit_bytes=56 << 20
        ),
        name="codistill",
    )(
        partners, frame_mask, segment_ids, master[0], moment_one[0], moment_two[0],
        hidden.reshape(frames, depth),
    )
    return hg.reshape(hidden.shape), new_master[None], m1[None], m2[None]


def solution(mesh):
    axes = ("zl", "co", "zh", "x", "y")
    torus = Mesh(mesh.devices.reshape(4, 2, 2, 4, 4), axes)
    rep, dp = ("zl", "co"), ("zh", "x", "y")
    in_specs = (
        P(None, rep, dp, None),
        P(),
        P(None, dp),
        P(None, dp),
        P(rep, dp, None),
        P(rep, dp, None),
        P(rep, dp, None),
    )
    out_specs = (
        P(None, rep, dp, None),
        P(rep, dp, None),
        P(rep, dp, None),
        P(rep, dp, None),
    )
    return jax.shard_map(
        per_device, mesh=torus, in_specs=in_specs, out_specs=out_specs, check_vma=False
    )
```

```python
import jax
import jax.numpy as jnp
from jax import lax
from jax.experimental import pallas as pl
from jax.experimental.pallas import tpu as pltpu
from jax.sharding import Mesh
from jax.sharding import PartitionSpec as P

MESH = pl.DeviceIdType.MESH
F32 = jnp.float32
BF16 = jnp.bfloat16
SEGS = 8
REPS = 8
LANES = 128
UNITS = 4
ROWS = 60
PAD = 64
GROUP = 4 * ROWS
WIDE = 4 * PAD


def packed_of(padded):
    block = sum(jnp.where(padded >= k * PAD, 1, 0) for k in (1, 2, 3))
    inside = padded - block * PAD
    return jnp.where(inside < ROWS, block * ROWS + inside, -1)


def spread(rows, offset):
    at = lax.broadcasted_iota(jnp.int32, (rows, WIDE), 0)
    to = packed_of(lax.broadcasted_iota(jnp.int32, (rows, WIDE), 1))
    return jnp.where((to >= 0) & (at == to + offset), 1.0, 0.0).astype(BF16)


def kernel(
    partners, mask, segs, master, hidden_hbm,
    hg_out, g_out,
    hid, hid_p, hid_t, hp, head, logits, sent, got_0, got_1, got_2, got_3, stage, other, scale, grad,
    dw, r1, s2, r2, s3, r3,
    local_sem, z_s, z_r, a_s, a_r, b_s, b_r, p1_s, p1_r, p2_s, p2_r,
    c_s, c_r, d_s, d_r, e_s, e_r,
):
    zl, co = lax.axis_index("zl"), lax.axis_index("co")
    zh, x, y = lax.axis_index("zh"), lax.axis_index("x"), lax.axis_index("y")
    me = zl * 2 + co
    tokens = hid.shape[0] // 2
    part = tokens // REPS
    got = (got_0, got_1, got_2, got_3)

    load = pltpu.make_async_copy(hidden_hbm, hid, local_sem)
    load.start()

    def rep_of(d):
        to = lax.rem(me + d, REPS)
        return to, {"zl": to // 2, "co": lax.rem(to, 2)}

    def near(axis, d):
        to = lax.rem((x if axis == "x" else y) + d, 4)
        return to, {axis: to}

    across = {"zh": 1 - zh}

    barrier = pltpu.get_barrier_semaphore()
    peers = [across] + [near(a, d)[1] for a in ("x", "y") for d in (1, 2, 3)]
    peers += [rep_of(d)[1] for d in range(1, REPS)]
    for peer in peers:
        pl.semaphore_signal(barrier, inc=1, device_id=peer, device_id_type=MESH)

    low = master[:, 0, :].astype(BF16)
    vocab = low.shape[1]
    for u in range(UNITS):
        cols = min(LANES, vocab - u * LANES)
        piece = low[:, u * LANES : u * LANES + cols]
        if cols < LANES:
            piece = jnp.concatenate([piece, jnp.zeros((ROWS, LANES - cols), BF16)], axis=1)
        piece = jnp.concatenate([piece, jnp.zeros((PAD - ROWS, LANES), BF16)], axis=0)
        hp[u, zh, x, y] = piece

    pl.semaphore_wait(barrier, len(peers))

    started = []

    def send(src, dst, send_sem, recv_sem, peer):
        copy = pltpu.make_async_remote_copy(
            src_ref=src, dst_ref=dst, send_sem=send_sem, recv_sem=recv_sem,
            device_id=peer, device_id_type=MESH,
        )
        copy.start()
        started.append(copy)
        return copy

    def first_leg(u, half, along_x, along_y):
        ref = hp.at[u, half, x, y]
        copies = []
        for d in (1, 2, 3):
            peer = {"x": lax.rem(x + d * along_x, 4), "y": lax.rem(y + d * along_y, 4)}
            copies.append(send(ref, ref, a_s.at[u, half, d - 1], a_r.at[u, half, d - 1], peer))
        return copies

    z_copies, near_copies, far_copies, last_copies = [], [], [], []
    for u in range(UNITS):
        ref = hp.at[u, zh, x, y]
        z_copies.append(send(ref, ref, z_s.at[u], z_r.at[u], across))
        near_copies.append(first_leg(u, zh, 1 - zh, zh))
    for u in range(UNITS):
        z_copies[u].wait_recv()
        far_copies.append(first_leg(u, 1 - zh, zh, 1 - zh))
    for u in range(UNITS):
        for copy in near_copies[u] + far_copies[u]:
            copy.wait_recv()
        group = []
        for half, axis in ((0, "y"), (1, "x")):
            ref = hp.at[u, 0, :, y] if half == 0 else hp.at[u, 1, x]
            for d in (1, 2, 3):
                group.append(
                    send(ref, ref, b_s.at[u, half, d - 1], b_r.at[u, half, d - 1], near(axis, d)[1])
                )
        last_copies.append(group)

    load.wait()
    for g in range(8):
        start = min(g * GROUP // LANES * LANES, hid.shape[1] - 3 * LANES)
        matrix = spread(3 * LANES, g * GROUP - start)

        @pl.loop(0, 4)
        def _(t):
            rows = pl.ds(pl.multiple_of(t * WIDE, WIDE), WIDE)
            block = jnp.dot(hid[rows, start : start + 3 * LANES], matrix, preferred_element_type=F32)
            hid_p[rows, g * WIDE : (g + 1) * WIDE] = block.astype(BF16)

    def forward(u):
        for copy in last_copies[u]:
            copy.wait_recv()

        @pl.loop(0, 4)
        def _(t):
            rows = pl.ds(pl.multiple_of(t * WIDE, WIDE), WIDE)
            weights = hp[u].reshape(8 * WIDE, LANES)
            block = jnp.dot(hid_p[rows, :], weights, preferred_element_type=F32).reshape(4, part, LANES)
            logits[u, pl.ds(lax.rem(t, 2) * 4, 4), t // 2] = block
            sent[u, pl.ds(lax.rem(t, 2) * 4, 4), t // 2] = block.astype(BF16)

        copies = []
        for d in range(1, REPS):
            to, peer = rep_of(d)
            copies.append(send(sent.at[u, to], got[u].at[me], p1_s.at[u, d - 1], p1_r.at[u, d - 1], peer))
        got[u][me] = sent[u, me]
        return copies

    def choose(u, copies):
        for copy in copies:
            copy.wait_recv()
        after = []
        for d in range(1, REPS):
            to, peer = rep_of(d)
            for m in range(2):
                stage[u, d - 1, m] = got[u][partners[m, to], m]
            after.append(
                send(stage.at[u, d - 1], other.at[u, me], p2_s.at[u, d - 1], p2_r.at[u, d - 1], peer)
            )
        for m in range(2):
            other[u, me, m] = got[u][partners[m, me], m]
        return after

    def backward(u, copies):
        lanes = slice(u * LANES, (u + 1) * LANES)
        for copy in copies:
            copy.wait_recv()

        @pl.loop(0, REPS)
        def _(k):
            for m in range(2):
                rows = pl.ds(pl.multiple_of((m * REPS + k) * part, part), part)
                diff = logits[u, k, m] - other[u, k, m].astype(F32)
                grad[rows, lanes] = (diff * scale[rows, :]).astype(BF16)

        @pl.loop(0, 8)
        def _(g):
            rows = pl.ds(pl.multiple_of(g * WIDE, WIDE), WIDE)
            block = jnp.dot(hid_t[rows, :], grad[:, lanes], preferred_element_type=F32)
            dw[u, g // 4, lax.rem(g, 4)] = block.astype(BF16).reshape(4, PAD, LANES)

        result = []
        for half, axis in ((0, "y"), (1, "x")):
            group = []
            for d in (1, 2, 3):
                to, peer = near(axis, d)
                ref = dw.at[u, 0, :, to] if half == 0 else dw.at[u, 1, to]
                group.append(
                    send(ref, r1.at[u, half, d - 1], c_s.at[u, half, d - 1], c_r.at[u, half, d - 1], peer)
                )
            result.append(group)
        return result

    def second(u, copies):
        result = []
        for half, axis in ((0, "x"), (1, "y")):
            for copy in copies[half]:
                copy.wait_recv()
            for k in range(4):
                own = dw[u, 0, k, y] if half == 0 else dw[u, 1, x, k]
                total = own.astype(F32)
                for d in range(3):
                    total = total + r1[u, half, d, k].astype(F32)
                s2[u, half, k] = total.astype(BF16)
            group = []
            for d in (1, 2, 3):
                to, peer = near(axis, d)
                group.append(
                    send(
                        s2.at[u, half, to], r2.at[u, half, d - 1],
                        d_s.at[u, half, d - 1], d_r.at[u, half, d - 1], peer,
                    )
                )
            result.append(group)
        return result

    def third(u, copies):
        for half in range(2):
            for copy in copies[half]:
                copy.wait_recv()
            total = s2[u, half, x if half == 0 else y].astype(F32)
            for d in range(3):
                total = total + r2[u, half, d].astype(F32)
            s3[u, half] = total.astype(BF16)
        return send(s3.at[u, 1 - zh], r3.at[u], e_s.at[u], e_r.at[u], across)

    def finish(u, copy):
        copy.wait_recv()
        cols = min(LANES, vocab - u * LANES)
        total = s3[u, zh].astype(F32) + r3[u].astype(F32)
        g_out[:, 0, u * LANES : u * LANES + cols] = total[:ROWS, :cols]

    def pack_head(u):
        matrix = spread(GROUP, 0)

        @pl.loop(0, 8)
        def _(g):
            rows = pl.ds(pl.multiple_of(g * GROUP, 16), GROUP)
            block = hp[u, g // 4, lax.rem(g, 4)].reshape(WIDE, LANES)
            head[rows, u * LANES : (u + 1) * LANES] = jnp.dot(
                matrix, block, preferred_element_type=F32
            ).astype(BF16)

    p1_0 = forward(0)
    p1_1 = forward(1)
    for m in range(2):
        valid = mask[m : m + 1, :].astype(F32)
        ids = segs[m : m + 1, :]
        onehot = (lax.broadcasted_iota(jnp.int32, (SEGS, tokens), 0) == ids).astype(F32)
        counts = jnp.sum(onehot * valid, axis=1, keepdims=True)
        per_frame = jnp.sum(onehot * counts, axis=0, keepdims=True)
        row = valid / jnp.maximum(per_frame, 1.0)
        scale[m * tokens : (m + 1) * tokens, :] = jnp.broadcast_to(row, (LANES, tokens)).T
    p2_0 = choose(0, p1_0)
    p1_2 = forward(2)

    @pl.loop(0, hid_t.shape[0] // LANES)
    def _(j):
        at = pl.ds(pl.multiple_of(j * LANES, LANES), LANES)
        hid_t[at, :] = hid_p[:, at].T

    p2_1 = choose(1, p1_1)
    p1_3 = forward(3)
    for u in range(UNITS):
        pack_head(u)
    c_0 = backward(0, p2_0)
    p2_2 = choose(2, p1_2)
    d_0 = second(0, c_0)
    c_1 = backward(1, p2_1)
    p2_3 = choose(3, p1_3)
    e_0 = third(0, d_0)
    d_1 = second(1, c_1)
    c_2 = backward(2, p2_2)
    e_1 = third(1, d_1)
    finish(0, e_0)
    d_2 = second(2, c_2)
    finish(1, e_1)
    c_3 = backward(3, p2_3)

    def hidden_gradient(t):
        rows = slice(t * WIDE, (t + 1) * WIDE)
        width = 3 * LANES

        @pl.loop(0, hid.shape[1] // width)
        def _(n):
            at = pl.ds(pl.multiple_of(n * width, LANES), width)
            block = lax.dot_general(
                grad[rows, :], head[at, :], (((1,), (1,)), ((), ())), preferred_element_type=F32
            )
            hg_out[rows, at] = block.astype(BF16)

    hidden_gradient(0)
    e_2 = third(2, d_2)
    hidden_gradient(1)
    d_3 = second(3, c_3)
    hidden_gradient(2)
    finish(2, e_2)
    e_3 = third(3, d_3)
    hidden_gradient(3)
    finish(3, e_3)

    for copy in started:
        copy.wait_send()


def per_device(hidden, partners, frame_mask, segment_ids, master, moment_one, moment_two):
    tokens, depth = hidden.shape[2:]
    frames = 2 * tokens
    part = tokens // REPS
    wide = UNITS * LANES
    padded = 8 * WIDE
    vocab = master.shape[2]
    vmem = pl.BlockSpec(memory_space=pltpu.VMEM)
    dma = pltpu.SemaphoreType.DMA
    exchange = (REPS, 2, part, LANES)
    hg, head_grad = pl.pallas_call(
        kernel,
        out_shape=(pltpu.VMEM((frames, depth), BF16), jax.ShapeDtypeStruct((ROWS, 1, vocab), F32)),
        in_specs=[pl.BlockSpec(memory_space=pltpu.SMEM)] + [vmem] * 3 + [pl.BlockSpec(memory_space=pl.ANY)],
        out_specs=(vmem, vmem),
        scratch_shapes=[
            pltpu.VMEM((frames, depth), BF16),
            pltpu.VMEM((frames, padded), BF16),
            pltpu.VMEM((padded, frames), BF16),
            pltpu.VMEM((UNITS, 2, 4, 4, PAD, LANES), BF16),
            pltpu.VMEM((depth, wide), BF16),
            pltpu.VMEM((UNITS, *exchange), F32),
            pltpu.VMEM((UNITS, *exchange), BF16),
            pltpu.VMEM(exchange, BF16),
            pltpu.VMEM(exchange, BF16),
            pltpu.VMEM(exchange, BF16),
            pltpu.VMEM(exchange, BF16),
            pltpu.VMEM((UNITS, REPS - 1, 2, part, LANES), BF16),
            pltpu.VMEM((UNITS, *exchange), BF16),
            pltpu.VMEM((frames, LANES), F32),
            pltpu.VMEM((frames, wide), BF16),
            pltpu.VMEM((UNITS, 2, 4, 4, PAD, LANES), BF16),
            pltpu.VMEM((UNITS, 2, 3, 4, PAD, LANES), BF16),
            pltpu.VMEM((UNITS, 2, 4, PAD, LANES), BF16),
            pltpu.VMEM((UNITS, 2, 3, PAD, LANES), BF16),
            pltpu.VMEM((UNITS, 2, PAD, LANES), BF16),
            pltpu.VMEM((UNITS, PAD, LANES), BF16),
            dma,
            dma((UNITS,)), dma((UNITS,)),
            dma((UNITS, 2, 3)), dma((UNITS, 2, 3)),
            dma((UNITS, 2, 3)), dma((UNITS, 2, 3)),
            dma((UNITS, 7)), dma((UNITS, 7)),
            dma((UNITS, 7)), dma((UNITS, 7)),
            dma((UNITS, 2, 3)), dma((UNITS, 2, 3)),
            dma((UNITS, 2, 3)), dma((UNITS, 2, 3)),
            dma((UNITS,)), dma((UNITS,)),
        ],
        compiler_params=pltpu.CompilerParams(
            collective_id=0, has_side_effects=True, vmem_limit_bytes=52 << 20
        ),
        name="codistill",
    )(
        partners, frame_mask, segment_ids, master.reshape(ROWS, 1, vocab), hidden.reshape(frames, depth),
    )
    head_grad = head_grad.reshape(master.shape)
    new_moment_one = 0.9 * moment_one + 0.1 * head_grad
    new_moment_two = 0.99 * moment_two + 0.01 * head_grad * head_grad
    new_master = master - 0.01 * new_moment_one / (jnp.sqrt(new_moment_two) + 1e-08)
    return hg.reshape(hidden.shape), new_master, new_moment_one, new_moment_two


def solution(mesh):
    axes = ("zl", "co", "zh", "x", "y")
    torus = Mesh(mesh.devices.reshape(4, 2, 2, 4, 4), axes)
    rep, dp = ("zl", "co"), ("zh", "x", "y")
    in_specs = (
        P(None, rep, dp, None),
        P(),
        P(None, dp),
        P(None, dp),
        P(rep, dp, None),
        P(rep, dp, None),
        P(rep, dp, None),
    )
    out_specs = (
        P(None, rep, dp, None),
        P(rep, dp, None),
        P(rep, dp, None),
        P(rep, dp, None),
    )
    return jax.shard_map(
        per_device, mesh=torus, in_specs=in_specs, out_specs=out_specs, check_vma=False
    )
```

```python
import jax
import jax.numpy as jnp
from jax import lax
from jax.experimental import pallas as pl
from jax.experimental.pallas import tpu as pltpu
from jax.sharding import Mesh
from jax.sharding import PartitionSpec as P

MESH = pl.DeviceIdType.MESH
F32 = jnp.float32
BF16 = jnp.bfloat16
SEGS = 8
REPS = 8
LANES = 128
UNITS = 4
ROWS = 60
PAD = 64
GROUP = 4 * ROWS
WIDE = 4 * PAD


def spread(rows, offset, stride):
    at = lax.broadcasted_iota(jnp.int32, (rows, WIDE), 0)
    to = lax.broadcasted_iota(jnp.int32, (rows, WIDE), 1)
    block = sum(jnp.where(to >= k * PAD, 1, 0) for k in (1, 2, 3))
    inside = to - block * PAD
    return jnp.where((inside < ROWS) & (at == offset + block * stride + inside), 1.0, 0.0).astype(BF16)


def kernel(
    partners, mask_hbm, segs_hbm, master_hbm, hidden_hbm,
    hg_out, g_out,
    mask, segs, master, hid, hid_p, hid_t, hp, head, logits, sent, got_0, got_1, got_2, got_3, stage, other, scale, grad,
    dw, r1, s2, r2, s3, r3,
    local_sem, z_s, z_r, a_s, a_r, b_s, b_r, p1_s, p1_r, p2_s, p2_r,
    c_s, c_r, d_s, d_r, e_s, e_r,
):
    zl, co = lax.axis_index("zl"), lax.axis_index("co")
    zh, x, y = lax.axis_index("zh"), lax.axis_index("x"), lax.axis_index("y")
    me = zl * 2 + co
    tokens = hid.shape[0] // 2
    part = tokens // REPS
    got = (got_0, got_1, got_2, got_3)

    def rep_of(d):
        to = lax.rem(me + d, REPS)
        return to, {"zl": to // 2, "co": lax.rem(to, 2)}

    def first_of(q):
        return x * (1 - q) + y * q

    def second_of(q):
        return y * (1 - q) + x * q

    def on_first(q, d):
        return lax.rem(first_of(q) + d, 4), {"x": lax.rem(x + d * (1 - q), 4), "y": lax.rem(y + d * q, 4)}

    def on_second(q, d):
        return lax.rem(second_of(q) + d, 4), {"x": lax.rem(x + d * q, 4), "y": lax.rem(y + d * (1 - q), 4)}

    across = {"zh": 1 - zh}

    barrier = pltpu.get_barrier_semaphore()
    peers = [across] + [side(0, d)[1] for side in (on_first, on_second) for d in (1, 2, 3)]
    peers += [rep_of(d)[1] for d in range(1, REPS)]
    for peer in peers:
        pl.semaphore_signal(barrier, inc=1, device_id=peer, device_id_type=MESH)

    loads = []
    for i, (src, dst) in enumerate(((master_hbm, master), (hidden_hbm, hid), (mask_hbm, mask), (segs_hbm, segs))):
        copy = pltpu.make_async_copy(src, dst, local_sem.at[i])
        copy.start()
        loads.append(copy)

    loads[0].wait()
    low = master[:, 0, :].astype(BF16)
    vocab = low.shape[1]
    for u in range(UNITS):
        cols = min(LANES, vocab - u * LANES)
        piece = low[:, u * LANES : u * LANES + cols]
        if cols < LANES:
            piece = jnp.concatenate([piece, jnp.zeros((ROWS, LANES - cols), BF16)], axis=1)
        piece = jnp.concatenate([piece, jnp.zeros((PAD - ROWS, LANES), BF16)], axis=0)
        hp[u, zh, first_of(zh), second_of(zh)] = piece

    pl.semaphore_wait(barrier, len(peers))

    started = []

    def send(src, dst, send_sem, recv_sem, peer):
        copy = pltpu.make_async_remote_copy(
            src_ref=src, dst_ref=dst, send_sem=send_sem, recv_sem=recv_sem,
            device_id=peer, device_id_type=MESH,
        )
        copy.start()
        started.append(copy)
        return copy

    def leg_one(q):
        ref = hp.at[:, q, first_of(q), second_of(q)]
        return [
            send(ref, ref, a_s.at[q, d - 1], a_r.at[q, d - 1], on_first(q, d)[1]) for d in (1, 2, 3)
        ]

    legs = {}

    def leg_two(q, far, k):
        lo, hi = ((0, 1), (1, 2), (2, 4))[k]
        ref = hp.at[lo:hi, q, :, second_of(q)]
        legs[far, k] = [
            send(ref, ref, b_s.at[q, k, d - 1], b_r.at[q, k, d - 1], on_second(q, d)[1]) for d in (1, 2, 3)
        ]

    def arrived(copies):
        for copy in copies:
            copy.wait_recv()

    def pad_hidden(q, k):
        if q == 0:
            width, begin, stride = 3 * LANES, k * GROUP, ROWS
        else:
            width, begin, stride = 8 * LANES, 4 * GROUP + k * ROWS, GROUP
        start = min(begin // LANES * LANES, hid.shape[1] - width)
        matrix = spread(width, begin - start, stride)
        to = (4 * q + k) * WIDE

        @pl.loop(0, 4)
        def _(t):
            rows = pl.ds(pl.multiple_of(t * WIDE, WIDE), WIDE)
            block = jnp.dot(hid[rows, start : start + width], matrix, preferred_element_type=F32)
            hid_p[rows, to : to + WIDE] = block.astype(BF16)

    near_q, far_q = zh, 1 - zh
    near_one = leg_one(near_q)
    own = hp.at[:, zh, first_of(zh), second_of(zh)]
    z_copy = send(own, own, z_s, z_r, across)
    loads[1].wait()
    pad_hidden(0, 0)
    arrived(near_one)
    leg_two(near_q, 0, 0)
    pad_hidden(0, 1)
    arrived([z_copy])
    far_one = leg_one(far_q)
    leg_two(near_q, 0, 1)
    pad_hidden(0, 2)
    pad_hidden(0, 3)
    arrived(far_one)
    leg_two(far_q, 1, 0)
    leg_two(far_q, 1, 1)
    leg_two(near_q, 0, 2)
    leg_two(far_q, 1, 2)
    for k in range(4):
        pad_hidden(1, k)

    def forward(u):
        if u < 3:
            arrived(legs[0, u] + legs[1, u])

        @pl.loop(0, 4)
        def _(t):
            rows = pl.ds(pl.multiple_of(t * WIDE, WIDE), WIDE)
            weights = hp[u].reshape(8 * WIDE, LANES)
            block = jnp.dot(hid_p[rows, :], weights, preferred_element_type=F32).reshape(4, part, LANES)
            logits[u, pl.ds(lax.rem(t, 2) * 4, 4), t // 2] = block
            sent[u, pl.ds(lax.rem(t, 2) * 4, 4), t // 2] = block.astype(BF16)

        copies = []
        for d in range(1, REPS):
            to, peer = rep_of(d)
            copies.append(send(sent.at[u, to], got[u].at[me], p1_s.at[u, d - 1], p1_r.at[u, d - 1], peer))
        got[u][me] = sent[u, me]
        return copies

    def choose(u, copies):
        arrived(copies)
        after = []
        for d in range(1, REPS):
            to, peer = rep_of(d)
            for m in range(2):
                stage[u, d - 1, m] = got[u][partners[m, to], m]
            after.append(
                send(stage.at[u, d - 1], other.at[u, me], p2_s.at[u, d - 1], p2_r.at[u, d - 1], peer)
            )
        for m in range(2):
            other[u, me, m] = got[u][partners[m, me], m]
        return after

    def backward(u, copies):
        lanes = slice(u * LANES, (u + 1) * LANES)
        arrived(copies)

        @pl.loop(0, REPS)
        def _(k):
            for m in range(2):
                rows = pl.ds(pl.multiple_of((m * REPS + k) * part, part), part)
                diff = logits[u, k, m] - other[u, k, m].astype(F32)
                grad[rows, lanes] = (diff * scale[rows, :]).astype(BF16)

        @pl.loop(0, 8)
        def _(g):
            rows = pl.ds(pl.multiple_of(g * WIDE, WIDE), WIDE)
            block = jnp.dot(hid_t[rows, :], grad[:, lanes], preferred_element_type=F32)
            dw[u, g // 4, lax.rem(g, 4)] = block.astype(BF16).reshape(4, PAD, LANES)

    groups = ((0, 2), (2, 3), (3, 4))

    def reduce_one(i):
        lo, hi = groups[i]
        result = []
        for q in range(2):
            copies = []
            for d in (1, 2, 3):
                to, peer = on_second(q, d)
                copies.append(
                    send(
                        dw.at[lo:hi, q, :, to], r1.at[q, d - 1, lo:hi],
                        c_s.at[i, q, d - 1], c_r.at[i, q, d - 1], peer,
                    )
                )
            result.append(copies)
        return result

    def reduce_two(i, before):
        lo, hi = groups[i]
        result = []
        for q in range(2):
            arrived(before[q])
            for u in range(lo, hi):
                for k in range(4):
                    total = dw[u, q, k, second_of(q)].astype(F32)
                    for d in range(3):
                        total = total + r1[q, d, u, k].astype(F32)
                    s2[u, q, k] = total.astype(BF16)
            copies = []
            for d in (1, 2, 3):
                to, peer = on_first(q, d)
                copies.append(
                    send(
                        s2.at[lo:hi, q, to], r2.at[q, d - 1, lo:hi],
                        d_s.at[i, q, d - 1], d_r.at[i, q, d - 1], peer,
                    )
                )
            result.append(copies)
        return result

    def reduce_three(i, before):
        lo, hi = groups[i]
        for q in range(2):
            arrived(before[q])
            for u in range(lo, hi):
                total = s2[u, q, first_of(q)].astype(F32)
                for d in range(3):
                    total = total + r2[q, d, u].astype(F32)
                s3[u, q] = total.astype(BF16)
        return send(s3.at[lo:hi, 1 - zh], r3.at[lo:hi], e_s.at[i], e_r.at[i], across)

    def finish(i, copy):
        lo, hi = groups[i]
        arrived([copy])
        for u in range(lo, hi):
            cols = min(LANES, vocab - u * LANES)
            total = s3[u, zh].astype(F32) + r3[u].astype(F32)
            g_out[:, 0, u * LANES : u * LANES + cols] = total[:ROWS, :cols]

    def pack_head(u):
        matrix = spread(GROUP, 0, ROWS)
        lanes = slice(u * LANES, (u + 1) * LANES)

        @pl.loop(0, 4)
        def _(k):
            for q in range(2):
                block = hp[u, 0, k] if q == 0 else hp[u, 1, :, k]
                block = jnp.dot(matrix, block.reshape(WIDE, LANES), preferred_element_type=F32)
                head[pl.ds(pl.multiple_of((4 * q + k) * GROUP, 16), GROUP), lanes] = block.astype(BF16)

    p1_0 = forward(0)
    p1_1 = forward(1)
    for load in loads[2:]:
        load.wait()
    for m in range(2):
        valid = mask[m : m + 1, :].astype(F32)
        ids = segs[m : m + 1, :]
        onehot = (lax.broadcasted_iota(jnp.int32, (SEGS, tokens), 0) == ids).astype(F32)
        counts = jnp.sum(onehot * valid, axis=1, keepdims=True)
        per_frame = jnp.sum(onehot * counts, axis=0, keepdims=True)
        row = valid / jnp.maximum(per_frame, 1.0)
        scale[m * tokens : (m + 1) * tokens, :] = jnp.broadcast_to(row, (LANES, tokens)).T
    p2_0 = choose(0, p1_0)
    p1_2 = forward(2)

    @pl.loop(0, hid_t.shape[0] // LANES)
    def _(j):
        at = pl.ds(pl.multiple_of(j * LANES, LANES), LANES)
        hid_t[at, :] = hid_p[:, at].T

    p2_1 = choose(1, p1_1)
    p1_3 = forward(3)
    for u in range(UNITS):
        pack_head(u)
    backward(0, p2_0)
    p2_2 = choose(2, p1_2)
    backward(1, p2_1)
    c_0 = reduce_one(0)
    p2_3 = choose(3, p1_3)
    d_0 = reduce_two(0, c_0)
    backward(2, p2_2)
    c_1 = reduce_one(1)
    e_0 = reduce_three(0, d_0)
    backward(3, p2_3)
    c_2 = reduce_one(2)
    d_1 = reduce_two(1, c_1)
    finish(0, e_0)

    def hidden_gradient(t):
        rows = slice(t * WIDE, (t + 1) * WIDE)
        width = 3 * LANES

        @pl.loop(0, hid.shape[1] // width)
        def _(n):
            at = pl.ds(pl.multiple_of(n * width, LANES), width)
            block = lax.dot_general(
                grad[rows, :], head[at, :], (((1,), (1,)), ((), ())), preferred_element_type=F32
            )
            hg_out[rows, at] = block.astype(BF16)

    hidden_gradient(0)
    e_1 = reduce_three(1, d_1)
    hidden_gradient(1)
    d_2 = reduce_two(2, c_2)
    hidden_gradient(2)
    finish(1, e_1)
    e_2 = reduce_three(2, d_2)
    hidden_gradient(3)
    finish(2, e_2)

    for copy in started:
        copy.wait_send()


def per_device(hidden, partners, frame_mask, segment_ids, master, moment_one, moment_two):
    tokens, depth = hidden.shape[2:]
    frames = 2 * tokens
    part = tokens // REPS
    wide = UNITS * LANES
    padded = 8 * WIDE
    vocab = master.shape[2]
    vmem = pl.BlockSpec(memory_space=pltpu.VMEM)
    dma = pltpu.SemaphoreType.DMA
    exchange = (REPS, 2, part, LANES)
    hg, head_grad = pl.pallas_call(
        kernel,
        out_shape=(pltpu.VMEM((frames, depth), BF16), jax.ShapeDtypeStruct((ROWS, 1, vocab), F32)),
        in_specs=[pl.BlockSpec(memory_space=pltpu.SMEM)] + [pl.BlockSpec(memory_space=pl.ANY)] * 4,
        out_specs=(vmem, vmem),
        scratch_shapes=[
            pltpu.VMEM((2, tokens), jnp.int32),
            pltpu.VMEM((2, tokens), jnp.int32),
            pltpu.VMEM((ROWS, 1, vocab), F32),
            pltpu.VMEM((frames, depth), BF16),
            pltpu.VMEM((frames, padded), BF16),
            pltpu.VMEM((padded, frames), BF16),
            pltpu.VMEM((UNITS, 2, 4, 4, PAD, LANES), BF16),
            pltpu.VMEM((depth, wide), BF16),
            pltpu.VMEM((UNITS, *exchange), F32),
            pltpu.VMEM((UNITS, *exchange), BF16),
            pltpu.VMEM(exchange, BF16),
            pltpu.VMEM(exchange, BF16),
            pltpu.VMEM(exchange, BF16),
            pltpu.VMEM(exchange, BF16),
            pltpu.VMEM((UNITS, REPS - 1, 2, part, LANES), BF16),
            pltpu.VMEM((UNITS, *exchange), BF16),
            pltpu.VMEM((frames, LANES), F32),
            pltpu.VMEM((frames, wide), BF16),
            pltpu.VMEM((UNITS, 2, 4, 4, PAD, LANES), BF16),
            pltpu.VMEM((2, 3, UNITS, 4, PAD, LANES), BF16),
            pltpu.VMEM((UNITS, 2, 4, PAD, LANES), BF16),
            pltpu.VMEM((2, 3, UNITS, PAD, LANES), BF16),
            pltpu.VMEM((UNITS, 2, PAD, LANES), BF16),
            pltpu.VMEM((UNITS, PAD, LANES), BF16),
            dma((4,)),
            dma, dma,
            dma((2, 3)), dma((2, 3)),
            dma((2, 3, 3)), dma((2, 3, 3)),
            dma((UNITS, 7)), dma((UNITS, 7)),
            dma((UNITS, 7)), dma((UNITS, 7)),
            dma((3, 2, 3)), dma((3, 2, 3)),
            dma((3, 2, 3)), dma((3, 2, 3)),
            dma((3,)), dma((3,)),
        ],
        compiler_params=pltpu.CompilerParams(
            collective_id=0, has_side_effects=True, vmem_limit_bytes=52 << 20
        ),
        name="codistill",
    )(
        partners, frame_mask, segment_ids, master.reshape(ROWS, 1, vocab), hidden.reshape(frames, depth),
    )
    head_grad = head_grad.reshape(master.shape)
    new_moment_one = 0.9 * moment_one + 0.1 * head_grad
    new_moment_two = 0.99 * moment_two + 0.01 * head_grad * head_grad
    new_master = master - 0.01 * new_moment_one / (jnp.sqrt(new_moment_two) + 1e-08)
    return hg.reshape(hidden.shape), new_master, new_moment_one, new_moment_two


def solution(mesh):
    axes = ("zl", "co", "zh", "x", "y")
    torus = Mesh(mesh.devices.reshape(4, 2, 2, 4, 4), axes)
    rep, dp = ("zl", "co"), ("zh", "x", "y")
    in_specs = (
        P(None, rep, dp, None),
        P(),
        P(None, dp),
        P(None, dp),
        P(rep, dp, None),
        P(rep, dp, None),
        P(rep, dp, None),
    )
    out_specs = (
        P(None, rep, dp, None),
        P(rep, dp, None),
        P(rep, dp, None),
        P(rep, dp, None),
    )
    return jax.shard_map(
        per_device, mesh=torus, in_specs=in_specs, out_specs=out_specs, check_vma=False
    )
```

```python
import jax
import jax.numpy as jnp
from jax import lax
from jax.experimental import pallas as pl
from jax.experimental.pallas import tpu as pltpu
from jax.sharding import Mesh
from jax.sharding import PartitionSpec as P

MESH = pl.DeviceIdType.MESH
F32 = jnp.float32
BF16 = jnp.bfloat16
SEGS = 8
REPS = 8
LANES = 128
UNITS = 4
ROWS = 60
PAD = 64
GROUP = 4 * ROWS
WIDE = 4 * PAD


def spread(transposed):
    shape = (WIDE, GROUP) if transposed else (GROUP, WIDE)
    packed = lax.broadcasted_iota(jnp.int32, shape, 1 if transposed else 0)
    padded = lax.broadcasted_iota(jnp.int32, shape, 0 if transposed else 1)
    moved = packed + sum(jnp.where(packed >= k * ROWS, PAD - ROWS, 0) for k in (1, 2, 3))
    return jnp.where(moved == padded, 1.0, 0.0).astype(BF16)


def kernel(
    partners, mask_hbm, segs_hbm, master_hbm, hidden_hbm,
    hg_out, g_out,
    mask, segs, master, hid, hid_t, hp, packing, growing, head, logits, sent, got_0, got_1, got_2, got_3, stage, other, scale, grad,
    dw, r1, s2, r2, s3, r3,
    local_sem, z_s, z_r, a_s, a_r, b_s, b_r, p1_s, p1_r, p2_s, p2_r,
    c_s, c_r, d_s, d_r, e_s, e_r,
):
    zl, co = lax.axis_index("zl"), lax.axis_index("co")
    zh, x, y = lax.axis_index("zh"), lax.axis_index("x"), lax.axis_index("y")
    me = zl * 2 + co
    tokens = hid.shape[0] // 2
    part = tokens // REPS
    got = (got_0, got_1, got_2, got_3)

    def rep_of(d):
        to = lax.rem(me + d, REPS)
        return to, {"zl": to // 2, "co": lax.rem(to, 2)}

    def first_of(q):
        return x * (1 - q) + y * q

    def second_of(q):
        return y * (1 - q) + x * q

    def on_first(q, d):
        return lax.rem(first_of(q) + d, 4), {"x": lax.rem(x + d * (1 - q), 4), "y": lax.rem(y + d * q, 4)}

    def on_second(q, d):
        return lax.rem(second_of(q) + d, 4), {"x": lax.rem(x + d * q, 4), "y": lax.rem(y + d * (1 - q), 4)}

    across = {"zh": 1 - zh}

    barrier = pltpu.get_barrier_semaphore()
    peers = [across] + [side(0, d)[1] for side in (on_first, on_second) for d in (1, 2, 3)]
    peers += [rep_of(d)[1] for d in range(1, REPS)]
    for peer in peers:
        pl.semaphore_signal(barrier, inc=1, device_id=peer, device_id_type=MESH)

    loads = []
    for i, (src, dst) in enumerate(((master_hbm, master), (hidden_hbm, hid), (mask_hbm, mask), (segs_hbm, segs))):
        copy = pltpu.make_async_copy(src, dst, local_sem.at[i])
        copy.start()
        loads.append(copy)

    loads[0].wait()
    low = master[:, 0, :].astype(BF16)
    vocab = low.shape[1]
    for u in range(UNITS):
        cols = min(LANES, vocab - u * LANES)
        piece = low[:, u * LANES : u * LANES + cols]
        if cols < LANES:
            piece = jnp.concatenate([piece, jnp.zeros((ROWS, LANES - cols), BF16)], axis=1)
        piece = jnp.concatenate([piece, jnp.zeros((PAD - ROWS, LANES), BF16)], axis=0)
        hp[u, zh, first_of(zh), second_of(zh)] = piece

    packing[...] = spread(False)
    growing[...] = spread(True)
    pl.semaphore_wait(barrier, len(peers))

    started = []

    def send(src, dst, send_sem, recv_sem, peer):
        copy = pltpu.make_async_remote_copy(
            src_ref=src, dst_ref=dst, send_sem=send_sem, recv_sem=recv_sem,
            device_id=peer, device_id_type=MESH,
        )
        copy.start()
        started.append(copy)
        return copy

    parts = ((0, 1), (1, UNITS))

    def leg_one(q, i):
        ref = hp.at[parts[i][0] : parts[i][1], q, first_of(q), second_of(q)]
        return [
            send(ref, ref, a_s.at[i, q, d - 1], a_r.at[i, q, d - 1], on_first(q, d)[1]) for d in (1, 2, 3)
        ]

    def leg_z(i):
        ref = hp.at[parts[i][0] : parts[i][1], zh, first_of(zh), second_of(zh)]
        return send(ref, ref, z_s.at[i], z_r.at[i], across)

    def leg_two(q, k):
        lo, hi = ((0, 1), (1, 2), (2, 4))[k]
        ref = hp.at[lo:hi, q, :, second_of(q)]
        return [
            send(ref, ref, b_s.at[q, k, d - 1], b_r.at[q, k, d - 1], on_second(q, d)[1]) for d in (1, 2, 3)
        ]

    def arrived(copies):
        for copy in copies:
            copy.wait_recv()

    def sent_all(count):
        for copy in started[:count]:
            copy.wait_send()
        del started[:count]

    near, far = zh, 1 - zh
    near_a = leg_one(near, 0)
    z_a = leg_z(0)
    near_b = leg_one(near, 1)
    z_b = leg_z(1)
    arrived(near_a)
    near_0 = leg_two(near, 0)
    arrived([z_a])
    far_a = leg_one(far, 0)
    arrived(near_b)
    near_1 = leg_two(near, 1)
    arrived(far_a)
    far_0 = leg_two(far, 0)
    arrived([z_b])
    far_b = leg_one(far, 1)
    loads[1].wait()

    def forward(u):
        lanes = slice(u * LANES, (u + 1) * LANES)
        for k in range(4):
            for q in range(2):
                block = hp[u, 0, k] if q == 0 else hp[u, 1, :, k]
                block = jnp.dot(packing[...], block.reshape(WIDE, LANES), preferred_element_type=F32)
                head[(4 * q + k) * GROUP : (4 * q + k + 1) * GROUP, lanes] = block.astype(BF16)

        @pl.loop(0, 2)
        def _(m):
            rows = pl.ds(pl.multiple_of(m * tokens, tokens), tokens)
            block = jnp.dot(hid[rows, :], head[:, lanes], preferred_element_type=F32)
            block = block.reshape(REPS, part, LANES)
            logits[u, :, m] = block
            sent[u, :, m] = block.astype(BF16)

        copies = []
        for d in range(1, REPS):
            to, peer = rep_of(d)
            copies.append(send(sent.at[u, to], got[u].at[me], p1_s.at[u, d - 1], p1_r.at[u, d - 1], peer))
        got[u][me] = sent[u, me]
        return copies

    def choose(u, copies):
        arrived(copies)
        after = []
        for d in range(1, REPS):
            to, peer = rep_of(d)
            for m in range(2):
                stage[u, d - 1, m] = got[u][partners[m, to], m]
            after.append(
                send(stage.at[u, d - 1], other.at[u, me], p2_s.at[u, d - 1], p2_r.at[u, d - 1], peer)
            )
        for m in range(2):
            other[u, me, m] = got[u][partners[m, me], m]
        return after

    def backward(u, copies):
        lanes = slice(u * LANES, (u + 1) * LANES)
        arrived(copies)

        @pl.loop(0, REPS)
        def _(k):
            for m in range(2):
                rows = pl.ds(pl.multiple_of((m * REPS + k) * part, part), part)
                diff = logits[u, k, m] - other[u, k, m].astype(F32)
                grad[rows, lanes] = (diff * scale[rows, :]).astype(BF16)

        for k in range(4):
            for q in range(2):
                rows = slice((4 * q + k) * GROUP, (4 * q + k + 1) * GROUP)
                block = jnp.dot(hid_t[rows, :], grad[:, lanes], preferred_element_type=F32).astype(BF16)
                block = jnp.dot(growing[...], block, preferred_element_type=F32).astype(BF16)
                if q == 0:
                    dw[u, 0, k] = block.reshape(4, PAD, LANES)
                else:
                    dw[u, 1, :, k] = block.reshape(4, PAD, LANES)

    groups = ((0, 2), (2, 3), (3, 4))

    def reduce_one(i):
        lo, hi = groups[i]
        result = []
        for q in range(2):
            copies = []
            for d in (1, 2, 3):
                to, peer = on_second(q, d)
                copies.append(
                    send(
                        dw.at[lo:hi, q, :, to], r1.at[q, d - 1, lo:hi],
                        c_s.at[i, q, d - 1], c_r.at[i, q, d - 1], peer,
                    )
                )
            result.append(copies)
        return result

    def reduce_two(i, before):
        lo, hi = groups[i]
        result = []
        for q in range(2):
            arrived(before[q])
            for u in range(lo, hi):
                for k in range(4):
                    total = dw[u, q, k, second_of(q)].astype(F32)
                    for d in range(3):
                        total = total + r1[q, d, u, k].astype(F32)
                    s2[u, q, k] = total.astype(BF16)
            copies = []
            for d in (1, 2, 3):
                to, peer = on_first(q, d)
                copies.append(
                    send(
                        s2.at[lo:hi, q, to], r2.at[q, d - 1, lo:hi],
                        d_s.at[i, q, d - 1], d_r.at[i, q, d - 1], peer,
                    )
                )
            result.append(copies)
        return result

    def reduce_three(i, before):
        lo, hi = groups[i]
        for q in range(2):
            arrived(before[q])
            for u in range(lo, hi):
                total = s2[u, q, first_of(q)].astype(F32)
                for d in range(3):
                    total = total + r2[q, d, u].astype(F32)
                s3[u, q] = total.astype(BF16)
        return send(s3.at[lo:hi, 1 - zh], r3.at[lo:hi], e_s.at[i], e_r.at[i], across)

    def finish(i, copy):
        lo, hi = groups[i]
        arrived([copy])
        for u in range(lo, hi):
            cols = min(LANES, vocab - u * LANES)
            total = s3[u, zh].astype(F32) + r3[u].astype(F32)
            g_out[:, 0, u * LANES : u * LANES + cols] = total[:ROWS, :cols]

    arrived(near_0 + far_0)
    arrived(far_b)
    far_1 = leg_two(far, 1)
    near_2 = leg_two(near, 2)
    p1_0 = forward(0)
    for load in loads[2:]:
        load.wait()
    for m in range(2):
        valid = mask[m : m + 1, :].astype(F32)
        ids = segs[m : m + 1, :]
        onehot = (lax.broadcasted_iota(jnp.int32, (SEGS, tokens), 0) == ids).astype(F32)
        counts = jnp.sum(onehot * valid, axis=1, keepdims=True)
        per_frame = jnp.sum(onehot * counts, axis=0, keepdims=True)
        row = valid / jnp.maximum(per_frame, 1.0)
        scale[m * tokens : (m + 1) * tokens, :] = jnp.broadcast_to(row, (LANES, tokens)).T
    arrived(near_1 + far_1)
    far_2 = leg_two(far, 2)
    p1_1 = forward(1)
    p2_0 = choose(0, p1_0)
    arrived(near_2 + far_2)
    p1_2 = forward(2)

    @pl.loop(0, hid_t.shape[0] // LANES)
    def _(j):
        at = pl.ds(pl.multiple_of(j * LANES, LANES), LANES)
        hid_t[at, :] = hid[:, at].T

    p2_1 = choose(1, p1_1)
    p1_3 = forward(3)
    early = len(started)
    backward(0, p2_0)
    p2_2 = choose(2, p1_2)
    backward(1, p2_1)
    c_0 = reduce_one(0)
    p2_3 = choose(3, p1_3)
    sent_all(early)
    d_0 = reduce_two(0, c_0)
    backward(2, p2_2)
    c_1 = reduce_one(1)
    e_0 = reduce_three(0, d_0)
    backward(3, p2_3)
    c_2 = reduce_one(2)
    d_1 = reduce_two(1, c_1)
    finish(0, e_0)

    def hidden_gradient(t):
        rows = slice(t * WIDE, (t + 1) * WIDE)
        width = 3 * LANES

        @pl.loop(0, hid.shape[1] // width)
        def _(n):
            at = pl.ds(pl.multiple_of(n * width, LANES), width)
            block = lax.dot_general(
                grad[rows, :], head[at, :], (((1,), (1,)), ((), ())), preferred_element_type=F32
            )
            hg_out[rows, at] = block.astype(BF16)

    hidden_gradient(0)
    e_1 = reduce_three(1, d_1)
    hidden_gradient(1)
    d_2 = reduce_two(2, c_2)
    hidden_gradient(2)
    finish(1, e_1)
    e_2 = reduce_three(2, d_2)
    hidden_gradient(3)
    finish(2, e_2)

    sent_all(len(started))


def per_device(hidden, partners, frame_mask, segment_ids, master, moment_one, moment_two):
    tokens, depth = hidden.shape[2:]
    frames = 2 * tokens
    part = tokens // REPS
    wide = UNITS * LANES
    vocab = master.shape[2]
    vmem = pl.BlockSpec(memory_space=pltpu.VMEM)
    dma = pltpu.SemaphoreType.DMA
    exchange = (REPS, 2, part, LANES)
    hg, head_grad = pl.pallas_call(
        kernel,
        out_shape=(pltpu.VMEM((frames, depth), BF16), jax.ShapeDtypeStruct((ROWS, 1, vocab), F32)),
        in_specs=[pl.BlockSpec(memory_space=pltpu.SMEM)] + [pl.BlockSpec(memory_space=pl.ANY)] * 4,
        out_specs=(vmem, vmem),
        scratch_shapes=[
            pltpu.VMEM((2, tokens), jnp.int32),
            pltpu.VMEM((2, tokens), jnp.int32),
            pltpu.VMEM((ROWS, 1, vocab), F32),
            pltpu.VMEM((frames, depth), BF16),
            pltpu.VMEM((depth, frames), BF16),
            pltpu.VMEM((UNITS, 2, 4, 4, PAD, LANES), BF16),
            pltpu.VMEM((GROUP, WIDE), BF16),
            pltpu.VMEM((WIDE, GROUP), BF16),
            pltpu.VMEM((depth, wide), BF16),
            pltpu.VMEM((UNITS, *exchange), F32),
            pltpu.VMEM((UNITS, *exchange), BF16),
            pltpu.VMEM(exchange, BF16),
            pltpu.VMEM(exchange, BF16),
            pltpu.VMEM(exchange, BF16),
            pltpu.VMEM(exchange, BF16),
            pltpu.VMEM((UNITS, REPS - 1, 2, part, LANES), BF16),
            pltpu.VMEM((UNITS, *exchange), BF16),
            pltpu.VMEM((frames, LANES), F32),
            pltpu.VMEM((frames, wide), BF16),
            pltpu.VMEM((UNITS, 2, 4, 4, PAD, LANES), BF16),
            pltpu.VMEM((2, 3, UNITS, 4, PAD, LANES), BF16),
            pltpu.VMEM((UNITS, 2, 4, PAD, LANES), BF16),
            pltpu.VMEM((2, 3, UNITS, PAD, LANES), BF16),
            pltpu.VMEM((UNITS, 2, PAD, LANES), BF16),
            pltpu.VMEM((UNITS, PAD, LANES), BF16),
            dma((4,)),
            dma((2,)), dma((2,)),
            dma((2, 2, 3)), dma((2, 2, 3)),
            dma((2, 3, 3)), dma((2, 3, 3)),
            dma((UNITS, 7)), dma((UNITS, 7)),
            dma((UNITS, 7)), dma((UNITS, 7)),
            dma((3, 2, 3)), dma((3, 2, 3)),
            dma((3, 2, 3)), dma((3, 2, 3)),
            dma((3,)), dma((3,)),
        ],
        compiler_params=pltpu.CompilerParams(
            collective_id=0, has_side_effects=True, vmem_limit_bytes=52 << 20
        ),
        name="codistill",
    )(
        partners, frame_mask, segment_ids, master.reshape(ROWS, 1, vocab), hidden.reshape(frames, depth),
    )
    head_grad = head_grad.reshape(master.shape)
    new_moment_one = 0.9 * moment_one + 0.1 * head_grad
    new_moment_two = 0.99 * moment_two + 0.01 * head_grad * head_grad
    new_master = master - 0.01 * new_moment_one / (jnp.sqrt(new_moment_two) + 1e-08)
    return hg.reshape(hidden.shape), new_master, new_moment_one, new_moment_two


def solution(mesh):
    axes = ("zl", "co", "zh", "x", "y")
    torus = Mesh(mesh.devices.reshape(4, 2, 2, 4, 4), axes)
    rep, dp = ("zl", "co"), ("zh", "x", "y")
    in_specs = (
        P(None, rep, dp, None),
        P(),
        P(None, dp),
        P(None, dp),
        P(rep, dp, None),
        P(rep, dp, None),
        P(rep, dp, None),
    )
    out_specs = (
        P(None, rep, dp, None),
        P(rep, dp, None),
        P(rep, dp, None),
        P(rep, dp, None),
    )
    return jax.shard_map(
        per_device, mesh=torus, in_specs=in_specs, out_specs=out_specs, check_vma=False
    )
```

```python
import jax
import jax.numpy as jnp
from jax import lax
from jax.experimental import pallas as pl
from jax.experimental.pallas import tpu as pltpu
from jax.sharding import Mesh
from jax.sharding import PartitionSpec as P

MESH = pl.DeviceIdType.MESH
F32 = jnp.float32
BF16 = jnp.bfloat16
SEGS = 8
REPS = 8
LANES = 128
UNITS = 4
ROWS = 60
PAD = 64
GROUP = 4 * ROWS
WIDE = 4 * PAD


def spread(transposed):
    shape = (WIDE, GROUP) if transposed else (GROUP, WIDE)
    packed = lax.broadcasted_iota(jnp.int32, shape, 1 if transposed else 0)
    padded = lax.broadcasted_iota(jnp.int32, shape, 0 if transposed else 1)
    moved = packed + sum(jnp.where(packed >= k * ROWS, PAD - ROWS, 0) for k in (1, 2, 3))
    return jnp.where(moved == padded, 1.0, 0.0).astype(BF16)


def kernel(
    partners_hbm, mask_hbm, segs_hbm, master_hbm, hidden_hbm,
    hg_out, g_out,
    partners, mask, segs, master, hid, hid_t, hp, packing, growing, head, logits, sent, got_0, got_1, got_2, got_3, stage, other, scale, grad,
    dw, r1, s2, r2, s3, r3,
    local_sem, z_s, z_r, a_s, a_r, b_s, b_r, p1_s, p1_r, p2_s, p2_r,
    c_s, c_r, d_s, d_r, e_s, e_r,
):
    zl, co = lax.axis_index("zl"), lax.axis_index("co")
    zh, x, y = lax.axis_index("zh"), lax.axis_index("x"), lax.axis_index("y")
    me = zl * 2 + co
    tokens = hid.shape[0] // 2
    part = tokens // REPS
    got = (got_0, got_1, got_2, got_3)

    def rep_of(d):
        to = lax.rem(me + d, REPS)
        return to, {"zl": to // 2, "co": lax.rem(to, 2)}

    def first_of(q):
        return x * (1 - q) + y * q

    def second_of(q):
        return y * (1 - q) + x * q

    def on_first(q, d):
        return lax.rem(first_of(q) + d, 4), {"x": lax.rem(x + d * (1 - q), 4), "y": lax.rem(y + d * q, 4)}

    def on_second(q, d):
        return lax.rem(second_of(q) + d, 4), {"x": lax.rem(x + d * q, 4), "y": lax.rem(y + d * (1 - q), 4)}

    across = {"zh": 1 - zh}

    barrier = pltpu.get_barrier_semaphore()
    peers = [across] + [side(0, d)[1] for side in (on_first, on_second) for d in (1, 2, 3)]
    peers += [rep_of(d)[1] for d in range(1, REPS)]
    for peer in peers:
        pl.semaphore_signal(barrier, inc=1, device_id=peer, device_id_type=MESH)

    loads = []
    for i, (src, dst) in enumerate(((master_hbm, master), (hidden_hbm, hid), (mask_hbm, mask), (segs_hbm, segs), (partners_hbm, partners))):
        copy = pltpu.make_async_copy(src, dst, local_sem.at[i])
        copy.start()
        loads.append(copy)

    loads[0].wait()
    low = master[:, 0, :].astype(BF16)
    vocab = low.shape[1]
    for u in range(UNITS):
        cols = min(LANES, vocab - u * LANES)
        piece = low[:, u * LANES : u * LANES + cols]
        if cols < LANES:
            piece = jnp.concatenate([piece, jnp.zeros((ROWS, LANES - cols), BF16)], axis=1)
        piece = jnp.concatenate([piece, jnp.zeros((PAD - ROWS, LANES), BF16)], axis=0)
        hp[u, zh, first_of(zh), second_of(zh)] = piece

    packing[...] = spread(False)
    growing[...] = spread(True)
    pl.semaphore_wait(barrier, len(peers))

    started = []

    def send(src, dst, send_sem, recv_sem, peer):
        copy = pltpu.make_async_remote_copy(
            src_ref=src, dst_ref=dst, send_sem=send_sem, recv_sem=recv_sem,
            device_id=peer, device_id_type=MESH,
        )
        copy.start()
        started.append(copy)
        return copy

    parts = ((0, 1), (1, UNITS))

    def leg_one(q, i):
        ref = hp.at[parts[i][0] : parts[i][1], q, first_of(q), second_of(q)]
        return [
            send(ref, ref, a_s.at[i, q, d - 1], a_r.at[i, q, d - 1], on_first(q, d)[1]) for d in (1, 2, 3)
        ]

    def leg_z(i):
        ref = hp.at[parts[i][0] : parts[i][1], zh, first_of(zh), second_of(zh)]
        return send(ref, ref, z_s.at[i], z_r.at[i], across)

    def leg_two(q, k):
        lo, hi = ((0, 1), (1, 2), (2, 4))[k]
        ref = hp.at[lo:hi, q, :, second_of(q)]
        return [
            send(ref, ref, b_s.at[q, k, d - 1], b_r.at[q, k, d - 1], on_second(q, d)[1]) for d in (1, 2, 3)
        ]

    def arrived(copies):
        for copy in copies:
            copy.wait_recv()

    def sent_all(count):
        for copy in started[:count]:
            copy.wait_send()
        del started[:count]

    near, far = zh, 1 - zh
    z_a = leg_z(0)
    near_a = leg_one(near, 0)
    z_b = leg_z(1)
    near_b = leg_one(near, 1)
    arrived(near_a)
    near_0 = leg_two(near, 0)
    loads[1].wait()
    arrived([z_a])
    far_a = leg_one(far, 0)
    arrived([z_b])
    far_b = leg_one(far, 1)
    arrived(far_a)
    far_0 = leg_two(far, 0)
    arrived(near_b)

    def forward(u):
        lanes = slice(u * LANES, (u + 1) * LANES)
        for k in range(4):
            for q in range(2):
                block = hp[u, 0, k] if q == 0 else hp[u, 1, :, k]
                block = jnp.dot(packing[...], block.reshape(WIDE, LANES), preferred_element_type=F32)
                head[(4 * q + k) * GROUP : (4 * q + k + 1) * GROUP, lanes] = block.astype(BF16)

        @pl.loop(0, 2)
        def _(m):
            rows = pl.ds(pl.multiple_of(m * tokens, tokens), tokens)
            block = jnp.dot(hid[rows, :], head[:, lanes], preferred_element_type=F32)
            block = block.reshape(REPS, part, LANES)
            logits[u, :, m] = block
            sent[u, :, m] = block.astype(BF16)

        copies = []
        for d in range(1, REPS):
            to, peer = rep_of(d)
            copies.append(send(sent.at[u, to], got[u].at[me], p1_s.at[u, d - 1], p1_r.at[u, d - 1], peer))
        got[u][me] = sent[u, me]
        return copies

    def choose(u, copies):
        arrived(copies)
        after = []
        for d in range(1, REPS):
            to, peer = rep_of(d)
            for m in range(2):
                stage[u, d - 1, m] = got[u][partners[m, to], m]
            after.append(
                send(stage.at[u, d - 1], other.at[u, me], p2_s.at[u, d - 1], p2_r.at[u, d - 1], peer)
            )
        for m in range(2):
            other[u, me, m] = got[u][partners[m, me], m]
        return after

    def backward(u, copies, then=None):
        lanes = slice(u * LANES, (u + 1) * LANES)
        result = []
        arrived(copies)

        @pl.loop(0, REPS)
        def _(k):
            for m in range(2):
                rows = pl.ds(pl.multiple_of((m * REPS + k) * part, part), part)
                diff = logits[u, k, m] - other[u, k, m].astype(F32)
                grad[rows, lanes] = (diff * scale[rows, :]).astype(BF16)

        for q in range(2):
            for k in range(4):
                rows = slice((4 * q + k) * GROUP, (4 * q + k + 1) * GROUP)
                block = jnp.dot(hid_t[rows, :], grad[:, lanes], preferred_element_type=F32).astype(BF16)
                block = jnp.dot(growing[...], block, preferred_element_type=F32).astype(BF16)
                if q == 0:
                    dw[u, 0, k] = block.reshape(4, PAD, LANES)
                else:
                    dw[u, 1, :, k] = block.reshape(4, PAD, LANES)
            if then is not None:
                result.append(then(q))
        return result

    groups = ((0, 2), (2, 3), (3, 4))

    def reduce_one(i):
        lo, hi = groups[i]

        def half(q):
            copies = []
            for d in (1, 2, 3):
                to, peer = on_second(q, d)
                copies.append(
                    send(
                        dw.at[lo:hi, q, :, to], r1.at[q, d - 1, lo:hi],
                        c_s.at[i, q, d - 1], c_r.at[i, q, d - 1], peer,
                    )
                )
            return copies

        return half

    def reduce_two(i, before):
        lo, hi = groups[i]
        result = []
        for q in range(2):
            arrived(before[q])
            for u in range(lo, hi):
                for k in range(4):
                    total = dw[u, q, k, second_of(q)].astype(F32)
                    for d in range(3):
                        total = total + r1[q, d, u, k].astype(F32)
                    s2[u, q, k] = total.astype(BF16)
            copies = []
            for d in (1, 2, 3):
                to, peer = on_first(q, d)
                copies.append(
                    send(
                        s2.at[lo:hi, q, to], r2.at[q, d - 1, lo:hi],
                        d_s.at[i, q, d - 1], d_r.at[i, q, d - 1], peer,
                    )
                )
            result.append(copies)
        return result

    def reduce_three(i, before):
        lo, hi = groups[i]
        arrived(before[0] + before[1])

        def sum_half(q):
            for u in range(lo, hi):
                total = s2[u, q, first_of(q)].astype(F32)
                for d in range(3):
                    total = total + r2[q, d, u].astype(F32)
                s3[u, q] = total.astype(BF16)

        sum_half(1 - zh)
        copy = send(s3.at[lo:hi, 1 - zh], r3.at[lo:hi], e_s.at[i], e_r.at[i], across)
        sum_half(zh)
        return copy

    def finish(i, copy):
        lo, hi = groups[i]
        arrived([copy])
        for u in range(lo, hi):
            cols = min(LANES, vocab - u * LANES)
            total = s3[u, zh].astype(F32) + r3[u].astype(F32)
            g_out[:, 0, u * LANES : u * LANES + cols] = total[:ROWS, :cols]

    arrived(near_0 + far_0)
    near_1 = leg_two(near, 1)
    p1_0 = forward(0)
    arrived(far_b)
    far_1 = leg_two(far, 1)
    near_2 = leg_two(near, 2)
    for load in loads[2:]:
        load.wait()
    for m in range(2):
        valid = mask[m : m + 1, :].astype(F32)
        ids = segs[m : m + 1, :]
        onehot = (lax.broadcasted_iota(jnp.int32, (SEGS, tokens), 0) == ids).astype(F32)
        counts = jnp.sum(onehot * valid, axis=1, keepdims=True)
        per_frame = jnp.sum(onehot * counts, axis=0, keepdims=True)
        row = valid / jnp.maximum(per_frame, 1.0)
        scale[m * tokens : (m + 1) * tokens, :] = jnp.broadcast_to(row, (LANES, tokens)).T
    arrived(near_1 + far_1)
    far_2 = leg_two(far, 2)
    p1_1 = forward(1)
    p2_0 = choose(0, p1_0)
    arrived(near_2 + far_2)
    p1_2 = forward(2)

    @pl.loop(0, hid_t.shape[0] // LANES)
    def _(j):
        at = pl.ds(pl.multiple_of(j * LANES, LANES), LANES)
        hid_t[at, :] = hid[:, at].T

    p2_1 = choose(1, p1_1)
    p1_3 = forward(3)
    early = len(started)
    backward(0, p2_0)
    p2_2 = choose(2, p1_2)
    c_0 = backward(1, p2_1, reduce_one(0))
    p2_3 = choose(3, p1_3)
    sent_all(early)
    d_0 = reduce_two(0, c_0)
    c_1 = backward(2, p2_2, reduce_one(1))
    e_0 = reduce_three(0, d_0)
    c_2 = backward(3, p2_3, reduce_one(2))
    d_1 = reduce_two(1, c_1)
    finish(0, e_0)

    def hidden_gradient(t):
        rows = slice(t * WIDE, (t + 1) * WIDE)
        width = 3 * LANES

        @pl.loop(0, hid.shape[1] // width)
        def _(n):
            at = pl.ds(pl.multiple_of(n * width, LANES), width)
            block = lax.dot_general(
                grad[rows, :], head[at, :], (((1,), (1,)), ((), ())), preferred_element_type=F32
            )
            hg_out[rows, at] = block.astype(BF16)

    hidden_gradient(0)
    e_1 = reduce_three(1, d_1)
    hidden_gradient(1)
    d_2 = reduce_two(2, c_2)
    hidden_gradient(2)
    finish(1, e_1)
    e_2 = reduce_three(2, d_2)
    hidden_gradient(3)
    finish(2, e_2)

    sent_all(len(started))


def per_device(hidden, partners, frame_mask, segment_ids, master, moment_one, moment_two):
    tokens, depth = hidden.shape[2:]
    frames = 2 * tokens
    part = tokens // REPS
    wide = UNITS * LANES
    vocab = master.shape[2]
    vmem = pl.BlockSpec(memory_space=pltpu.VMEM)
    dma = pltpu.SemaphoreType.DMA
    exchange = (REPS, 2, part, LANES)
    hg, head_grad = pl.pallas_call(
        kernel,
        out_shape=(pltpu.VMEM((frames, depth), BF16), jax.ShapeDtypeStruct((ROWS, 1, vocab), F32)),
        in_specs=[pl.BlockSpec(memory_space=pl.ANY)] * 5,
        out_specs=(vmem, vmem),
        scratch_shapes=[
            pltpu.SMEM((2, REPS), jnp.int32),
            pltpu.VMEM((2, tokens), jnp.int32),
            pltpu.VMEM((2, tokens), jnp.int32),
            pltpu.VMEM((ROWS, 1, vocab), F32),
            pltpu.VMEM((frames, depth), BF16),
            pltpu.VMEM((depth, frames), BF16),
            pltpu.VMEM((UNITS, 2, 4, 4, PAD, LANES), BF16),
            pltpu.VMEM((GROUP, WIDE), BF16),
            pltpu.VMEM((WIDE, GROUP), BF16),
            pltpu.VMEM((depth, wide), BF16),
            pltpu.VMEM((UNITS, *exchange), F32),
            pltpu.VMEM((UNITS, *exchange), BF16),
            pltpu.VMEM(exchange, BF16),
            pltpu.VMEM(exchange, BF16),
            pltpu.VMEM(exchange, BF16),
            pltpu.VMEM(exchange, BF16),
            pltpu.VMEM((UNITS, REPS - 1, 2, part, LANES), BF16),
            pltpu.VMEM((UNITS, *exchange), BF16),
            pltpu.VMEM((frames, LANES), F32),
            pltpu.VMEM((frames, wide), BF16),
            pltpu.VMEM((UNITS, 2, 4, 4, PAD, LANES), BF16),
            pltpu.VMEM((2, 3, UNITS, 4, PAD, LANES), BF16),
            pltpu.VMEM((UNITS, 2, 4, PAD, LANES), BF16),
            pltpu.VMEM((2, 3, UNITS, PAD, LANES), BF16),
            pltpu.VMEM((UNITS, 2, PAD, LANES), BF16),
            pltpu.VMEM((UNITS, PAD, LANES), BF16),
            dma((5,)),
            dma((2,)), dma((2,)),
            dma((2, 2, 3)), dma((2, 2, 3)),
            dma((2, 3, 3)), dma((2, 3, 3)),
            dma((UNITS, 7)), dma((UNITS, 7)),
            dma((UNITS, 7)), dma((UNITS, 7)),
            dma((3, 2, 3)), dma((3, 2, 3)),
            dma((3, 2, 3)), dma((3, 2, 3)),
            dma((3,)), dma((3,)),
        ],
        compiler_params=pltpu.CompilerParams(
            collective_id=0, has_side_effects=True, vmem_limit_bytes=52 << 20
        ),
        name="codistill",
    )(
        partners, frame_mask, segment_ids, master.reshape(ROWS, 1, vocab), hidden.reshape(frames, depth),
    )
    head_grad = head_grad.reshape(master.shape)
    new_moment_one = 0.9 * moment_one + 0.1 * head_grad
    new_moment_two = 0.99 * moment_two + 0.01 * head_grad * head_grad
    new_master = master - 0.01 * new_moment_one / (jnp.sqrt(new_moment_two) + 1e-08)
    return hg.reshape(hidden.shape), new_master, new_moment_one, new_moment_two


def solution(mesh):
    axes = ("zl", "co", "zh", "x", "y")
    torus = Mesh(mesh.devices.reshape(4, 2, 2, 4, 4), axes)
    rep, dp = ("zl", "co"), ("zh", "x", "y")
    in_specs = (
        P(None, rep, dp, None),
        P(),
        P(None, dp),
        P(None, dp),
        P(rep, dp, None),
        P(rep, dp, None),
        P(rep, dp, None),
    )
    out_specs = (
        P(None, rep, dp, None),
        P(rep, dp, None),
        P(rep, dp, None),
        P(rep, dp, None),
    )
    return jax.shard_map(
        per_device, mesh=torus, in_specs=in_specs, out_specs=out_specs, check_vma=False
    )
```

```python
import jax
import jax.numpy as jnp
from jax import lax
from jax.experimental import pallas as pl
from jax.experimental.pallas import tpu as pltpu
from jax.sharding import Mesh
from jax.sharding import PartitionSpec as P

MESH = pl.DeviceIdType.MESH
F32 = jnp.float32
BF16 = jnp.bfloat16
SEGS = 8
REPS = 8
LANES = 128
UNITS = 4
ROWS = 60
PAD = 64
GROUP = 4 * ROWS
WIDE = 4 * PAD


def spread(transposed):
    shape = (WIDE, GROUP) if transposed else (GROUP, WIDE)
    packed = lax.broadcasted_iota(jnp.int32, shape, 1 if transposed else 0)
    padded = lax.broadcasted_iota(jnp.int32, shape, 0 if transposed else 1)
    moved = packed + sum(jnp.where(packed >= k * ROWS, PAD - ROWS, 0) for k in (1, 2, 3))
    return jnp.where(moved == padded, 1.0, 0.0).astype(BF16)


def kernel(
    partners_hbm, mask_hbm, segs_hbm, master_hbm, hidden_hbm,
    hg_out, g_out,
    partners, mask, segs, master, hid, hid_t, hp, packing, growing, head, logits, sent, got_0, got_1, got_2, got_3, stage, other, scale, grad,
    dw, r1, s2, r2, s3, r3,
    local_sem, z_s, z_r, a_s, a_r, b_s, b_r, p1_s, p1_r, p2_s, p2_r,
    c_s, c_r, d_s, d_r, e_s, e_r,
):
    zl, co = lax.axis_index("zl"), lax.axis_index("co")
    zh, x, y = lax.axis_index("zh"), lax.axis_index("x"), lax.axis_index("y")
    me = zl * 2 + co
    tokens = hid.shape[0] // 2
    part = tokens // REPS
    got = (got_0, got_1, got_2, got_3)

    def rep_of(d):
        to = lax.rem(me + d, REPS)
        return to, {"zl": to // 2, "co": lax.rem(to, 2)}

    def first_of(q):
        return x * (1 - q) + y * q

    def second_of(q):
        return y * (1 - q) + x * q

    def on_first(q, d):
        return lax.rem(first_of(q) + d, 4), {"x": lax.rem(x + d * (1 - q), 4), "y": lax.rem(y + d * q, 4)}

    def on_second(q, d):
        return lax.rem(second_of(q) + d, 4), {"x": lax.rem(x + d * q, 4), "y": lax.rem(y + d * (1 - q), 4)}

    across = {"zh": 1 - zh}

    barrier = pltpu.get_barrier_semaphore()
    peers = [across] + [side(0, d)[1] for side in (on_first, on_second) for d in (1, 2, 3)]
    peers += [rep_of(d)[1] for d in range(1, REPS)]
    for peer in peers:
        pl.semaphore_signal(barrier, inc=1, device_id=peer, device_id_type=MESH)

    loads = []
    for i, (src, dst) in enumerate(((master_hbm, master), (hidden_hbm, hid), (mask_hbm, mask), (segs_hbm, segs), (partners_hbm, partners))):
        copy = pltpu.make_async_copy(src, dst, local_sem.at[i])
        copy.start()
        loads.append(copy)

    loads[0].wait()
    low = master[:, 0, :].astype(BF16)
    vocab = low.shape[1]
    for u in range(UNITS):
        cols = min(LANES, vocab - u * LANES)
        piece = low[:, u * LANES : u * LANES + cols]
        if cols < LANES:
            piece = jnp.concatenate([piece, jnp.zeros((ROWS, LANES - cols), BF16)], axis=1)
        piece = jnp.concatenate([piece, jnp.zeros((PAD - ROWS, LANES), BF16)], axis=0)
        hp[u, zh, first_of(zh), second_of(zh)] = piece

    packing[...] = spread(False)
    growing[...] = spread(True)
    pl.semaphore_wait(barrier, len(peers))

    started = []

    def send(src, dst, send_sem, recv_sem, peer):
        copy = pltpu.make_async_remote_copy(
            src_ref=src, dst_ref=dst, send_sem=send_sem, recv_sem=recv_sem,
            device_id=peer, device_id_type=MESH,
        )
        copy.start()
        started.append(copy)
        return copy

    parts = ((0, 1), (1, UNITS))

    def leg_one(q, i):
        ref = hp.at[parts[i][0] : parts[i][1], q, first_of(q), second_of(q)]
        return [
            send(ref, ref, a_s.at[i, q, d - 1], a_r.at[i, q, d - 1], on_first(q, d)[1]) for d in (1, 2, 3)
        ]

    def leg_z(i):
        ref = hp.at[parts[i][0] : parts[i][1], zh, first_of(zh), second_of(zh)]
        return send(ref, ref, z_s.at[i], z_r.at[i], across)

    def leg_two(q, k):
        lo, hi = ((0, 1), (1, 2), (2, 4))[k]
        ref = hp.at[lo:hi, q, :, second_of(q)]
        return [
            send(ref, ref, b_s.at[q, k, d - 1], b_r.at[q, k, d - 1], on_second(q, d)[1]) for d in (1, 2, 3)
        ]

    def arrived(copies):
        for copy in copies:
            copy.wait_recv()

    def sent_all(count):
        for copy in started[:count]:
            copy.wait_send()
        del started[:count]

    near, far = zh, 1 - zh
    z_a = leg_z(0)
    near_a = leg_one(near, 0)
    arrived(near_a)
    near_0 = leg_two(near, 0)
    loads[1].wait()
    arrived([z_a])
    far_a = leg_one(far, 0)
    z_b = leg_z(1)
    near_b = leg_one(near, 1)
    arrived(far_a)
    far_0 = leg_two(far, 0)
    arrived([z_b])
    far_b = leg_one(far, 1)
    arrived(near_b)

    def forward(u):
        lanes = slice(u * LANES, (u + 1) * LANES)
        for k in range(4):
            for q in range(2):
                block = hp[u, 0, k] if q == 0 else hp[u, 1, :, k]
                block = jnp.dot(packing[...], block.reshape(WIDE, LANES), preferred_element_type=F32)
                head[(4 * q + k) * GROUP : (4 * q + k + 1) * GROUP, lanes] = block.astype(BF16)

        @pl.loop(0, 2)
        def _(m):
            rows = pl.ds(pl.multiple_of(m * tokens, tokens), tokens)
            block = jnp.dot(hid[rows, :], head[:, lanes], preferred_element_type=F32)
            block = block.reshape(REPS, part, LANES)
            logits[u, :, m] = block
            sent[u, :, m] = block.astype(BF16)

        copies = []
        for d in range(1, REPS):
            to, peer = rep_of(d)
            copies.append(send(sent.at[u, to], got[u].at[me], p1_s.at[u, d - 1], p1_r.at[u, d - 1], peer))
        got[u][me] = sent[u, me]
        return copies

    def choose(u, copies):
        arrived(copies)
        after = []
        for d in range(1, REPS):
            to, peer = rep_of(d)
            for m in range(2):
                stage[u, d - 1, m] = got[u][partners[m, to], m]
            after.append(
                send(stage.at[u, d - 1], other.at[u, me], p2_s.at[u, d - 1], p2_r.at[u, d - 1], peer)
            )
        for m in range(2):
            other[u, me, m] = got[u][partners[m, me], m]
        return after

    def backward(u, copies, then=None):
        lanes = slice(u * LANES, (u + 1) * LANES)
        result = []
        arrived(copies)

        @pl.loop(0, REPS)
        def _(k):
            for m in range(2):
                rows = pl.ds(pl.multiple_of((m * REPS + k) * part, part), part)
                diff = logits[u, k, m] - other[u, k, m].astype(F32)
                grad[rows, lanes] = (diff * scale[rows, :]).astype(BF16)

        for q in range(2):
            for k in range(4):
                rows = slice((4 * q + k) * GROUP, (4 * q + k + 1) * GROUP)
                block = jnp.dot(hid_t[rows, :], grad[:, lanes], preferred_element_type=F32).astype(BF16)
                block = jnp.dot(growing[...], block, preferred_element_type=F32).astype(BF16)
                if q == 0:
                    dw[u, 0, k] = block.reshape(4, PAD, LANES)
                else:
                    dw[u, 1, :, k] = block.reshape(4, PAD, LANES)
            if then is not None:
                result.append(then(q))
        return result

    groups = ((0, 2), (2, 3), (3, 4))

    def reduce_one(i):
        lo, hi = groups[i]

        def half(q):
            copies = []
            for d in (1, 2, 3):
                to, peer = on_second(q, d)
                copies.append(
                    send(
                        dw.at[lo:hi, q, :, to], r1.at[q, d - 1, lo:hi],
                        c_s.at[i, q, d - 1], c_r.at[i, q, d - 1], peer,
                    )
                )
            return copies

        return half

    def reduce_two(i, before):
        lo, hi = groups[i]
        result = []
        for q in range(2):
            arrived(before[q])
            for u in range(lo, hi):
                for k in range(4):
                    total = dw[u, q, k, second_of(q)].astype(F32)
                    for d in range(3):
                        total = total + r1[q, d, u, k].astype(F32)
                    s2[u, q, k] = total.astype(BF16)
            copies = []
            for d in (1, 2, 3):
                to, peer = on_first(q, d)
                copies.append(
                    send(
                        s2.at[lo:hi, q, to], r2.at[q, d - 1, lo:hi],
                        d_s.at[i, q, d - 1], d_r.at[i, q, d - 1], peer,
                    )
                )
            result.append(copies)
        return result

    def reduce_three(i, before):
        lo, hi = groups[i]
        arrived(before[0] + before[1])

        def sum_half(q):
            for u in range(lo, hi):
                total = s2[u, q, first_of(q)].astype(F32)
                for d in range(3):
                    total = total + r2[q, d, u].astype(F32)
                s3[u, q] = total.astype(BF16)

        sum_half(1 - zh)
        copy = send(s3.at[lo:hi, 1 - zh], r3.at[lo:hi], e_s.at[i], e_r.at[i], across)
        sum_half(zh)
        return copy

    def finish(i, copy):
        lo, hi = groups[i]
        arrived([copy])
        for u in range(lo, hi):
            cols = min(LANES, vocab - u * LANES)
            total = s3[u, zh].astype(F32) + r3[u].astype(F32)
            g_out[:, 0, u * LANES : u * LANES + cols] = total[:ROWS, :cols]

    arrived(near_0 + far_0)
    near_1 = leg_two(near, 1)
    p1_0 = forward(0)
    arrived(far_b)
    far_1 = leg_two(far, 1)
    near_2 = leg_two(near, 2)
    for load in loads[2:]:
        load.wait()
    for m in range(2):
        valid = mask[m : m + 1, :].astype(F32)
        ids = segs[m : m + 1, :]
        onehot = (lax.broadcasted_iota(jnp.int32, (SEGS, tokens), 0) == ids).astype(F32)
        counts = jnp.sum(onehot * valid, axis=1, keepdims=True)
        per_frame = jnp.sum(onehot * counts, axis=0, keepdims=True)
        row = valid / jnp.maximum(per_frame, 1.0)
        scale[m * tokens : (m + 1) * tokens, :] = jnp.broadcast_to(row, (LANES, tokens)).T
    arrived(near_1 + far_1)
    far_2 = leg_two(far, 2)
    p1_1 = forward(1)
    p2_0 = choose(0, p1_0)
    arrived(near_2 + far_2)
    p1_2 = forward(2)

    @pl.loop(0, hid_t.shape[0] // LANES)
    def _(j):
        at = pl.ds(pl.multiple_of(j * LANES, LANES), LANES)
        hid_t[at, :] = hid[:, at].T

    p2_1 = choose(1, p1_1)
    p1_3 = forward(3)
    early = len(started)
    backward(0, p2_0)
    p2_2 = choose(2, p1_2)
    c_0 = backward(1, p2_1, reduce_one(0))
    p2_3 = choose(3, p1_3)
    sent_all(early)
    d_0 = reduce_two(0, c_0)
    c_1 = backward(2, p2_2, reduce_one(1))
    e_0 = reduce_three(0, d_0)
    c_2 = backward(3, p2_3, reduce_one(2))
    d_1 = reduce_two(1, c_1)

    def hidden_gradient(t):
        rows = slice(t * WIDE, (t + 1) * WIDE)
        width = 3 * LANES

        @pl.loop(0, hid.shape[1] // width)
        def _(n):
            at = pl.ds(pl.multiple_of(n * width, LANES), width)
            block = lax.dot_general(
                grad[rows, :], head[at, :], (((1,), (1,)), ((), ())), preferred_element_type=F32
            )
            hg_out[rows, at] = block.astype(BF16)

    hidden_gradient(0)
    hidden_gradient(1)
    hidden_gradient(2)
    d_2 = reduce_two(2, c_2)
    e_1 = reduce_three(1, d_1)
    hidden_gradient(3)
    e_2 = reduce_three(2, d_2)
    finish(0, e_0)
    finish(1, e_1)
    sent_all(len(started))
    finish(2, e_2)


def adam(hg, head_grad, master, moment_one, moment_two, hg_out, new_master, new_m1, new_m2, held, sems):
    height = hg.shape[0] // 4
    for t in range(4):
        rows = pl.ds(t * height, height)
        pltpu.make_async_copy(hg.at[rows], hg_out.at[rows], sems.at[7 + t]).start()
    loads = [
        pltpu.make_async_copy(ref, held.at[i], sems.at[i])
        for i, ref in enumerate((head_grad, master, moment_one, moment_two))
    ]
    for load in loads:
        load.start()
    for load in loads:
        load.wait()
    g = held[0]
    one = 0.9 * held[2] + 0.1 * g
    two = 0.99 * held[3] + 0.01 * g * g
    held[5] = one
    held[6] = two
    held[4] = held[1] - 0.01 * one / (jnp.sqrt(two) + 1e-08)
    stores = [
        pltpu.make_async_copy(held.at[4 + i], ref, sems.at[4 + i])
        for i, ref in enumerate((new_master, new_m1, new_m2))
    ]
    for store in stores:
        store.start()
    for store in stores:
        store.wait()
    for t in range(4):
        rows = pl.ds(t * height, height)
        pltpu.make_async_copy(hg.at[rows], hg_out.at[rows], sems.at[7 + t]).wait()


def per_device(hidden, partners, frame_mask, segment_ids, master, moment_one, moment_two):
    tokens, depth = hidden.shape[2:]
    frames = 2 * tokens
    part = tokens // REPS
    wide = UNITS * LANES
    vocab = master.shape[2]
    vmem = pl.BlockSpec(memory_space=pltpu.VMEM)
    hbm = pl.BlockSpec(memory_space=pl.ANY)
    dma = pltpu.SemaphoreType.DMA
    exchange = (REPS, 2, part, LANES)
    hg, head_grad = pl.pallas_call(
        kernel,
        out_shape=(pltpu.VMEM((frames, depth), BF16), pltpu.VMEM((ROWS, 1, vocab), F32)),
        in_specs=[pl.BlockSpec(memory_space=pl.ANY)] * 5,
        out_specs=(vmem, vmem),
        scratch_shapes=[
            pltpu.SMEM((2, REPS), jnp.int32),
            pltpu.VMEM((2, tokens), jnp.int32),
            pltpu.VMEM((2, tokens), jnp.int32),
            pltpu.VMEM((ROWS, 1, vocab), F32),
            pltpu.VMEM((frames, depth), BF16),
            pltpu.VMEM((depth, frames), BF16),
            pltpu.VMEM((UNITS, 2, 4, 4, PAD, LANES), BF16),
            pltpu.VMEM((GROUP, WIDE), BF16),
            pltpu.VMEM((WIDE, GROUP), BF16),
            pltpu.VMEM((depth, wide), BF16),
            pltpu.VMEM((UNITS, *exchange), F32),
            pltpu.VMEM((UNITS, *exchange), BF16),
            pltpu.VMEM(exchange, BF16),
            pltpu.VMEM(exchange, BF16),
            pltpu.VMEM(exchange, BF16),
            pltpu.VMEM(exchange, BF16),
            pltpu.VMEM((UNITS, REPS - 1, 2, part, LANES), BF16),
            pltpu.VMEM((UNITS, *exchange), BF16),
            pltpu.VMEM((frames, LANES), F32),
            pltpu.VMEM((frames, wide), BF16),
            pltpu.VMEM((UNITS, 2, 4, 4, PAD, LANES), BF16),
            pltpu.VMEM((2, 3, UNITS, 4, PAD, LANES), BF16),
            pltpu.VMEM((UNITS, 2, 4, PAD, LANES), BF16),
            pltpu.VMEM((2, 3, UNITS, PAD, LANES), BF16),
            pltpu.VMEM((UNITS, 2, PAD, LANES), BF16),
            pltpu.VMEM((UNITS, PAD, LANES), BF16),
            dma((5,)),
            dma((2,)), dma((2,)),
            dma((2, 2, 3)), dma((2, 2, 3)),
            dma((2, 3, 3)), dma((2, 3, 3)),
            dma((UNITS, 7)), dma((UNITS, 7)),
            dma((UNITS, 7)), dma((UNITS, 7)),
            dma((3, 2, 3)), dma((3, 2, 3)),
            dma((3, 2, 3)), dma((3, 2, 3)),
            dma((3,)), dma((3,)),
        ],
        compiler_params=pltpu.CompilerParams(
            collective_id=0, has_side_effects=True, vmem_limit_bytes=52 << 20
        ),
        name="codistill",
    )(
        partners, frame_mask, segment_ids, master.reshape(ROWS, 1, vocab), hidden.reshape(frames, depth),
    )
    flat = (ROWS, 1, vocab)
    small = jax.ShapeDtypeStruct(flat, F32)
    hg, new_master, new_m1, new_m2 = pl.pallas_call(
        adam,
        out_shape=(jax.ShapeDtypeStruct(hg.shape, BF16), small, small, small),
        in_specs=[hbm] * 5,
        out_specs=(hbm,) * 4,
        scratch_shapes=[pltpu.VMEM((7, *flat), F32), dma((11,))],
        compiler_params=pltpu.CompilerParams(vmem_limit_bytes=8 << 20),
        name="adam",
    )(hg, head_grad, master.reshape(flat), moment_one.reshape(flat), moment_two.reshape(flat))
    shape = master.shape
    return hg.reshape(hidden.shape), new_master.reshape(shape), new_m1.reshape(shape), new_m2.reshape(shape)


def solution(mesh):
    axes = ("zl", "co", "zh", "x", "y")
    torus = Mesh(mesh.devices.reshape(4, 2, 2, 4, 4), axes)
    rep, dp = ("zl", "co"), ("zh", "x", "y")
    in_specs = (
        P(None, rep, dp, None),
        P(),
        P(None, dp),
        P(None, dp),
        P(rep, dp, None),
        P(rep, dp, None),
        P(rep, dp, None),
    )
    out_specs = (
        P(None, rep, dp, None),
        P(rep, dp, None),
        P(rep, dp, None),
        P(rep, dp, None),
    )
    return jax.shard_map(
        per_device, mesh=torus, in_specs=in_specs, out_specs=out_specs, check_vma=False
    )
```

```python
import jax
import jax.numpy as jnp
from jax import lax
from jax.experimental import pallas as pl
from jax.experimental.pallas import tpu as pltpu
from jax.sharding import Mesh
from jax.sharding import PartitionSpec as P

MESH = pl.DeviceIdType.MESH
F32 = jnp.float32
BF16 = jnp.bfloat16
SEGS = 8
REPS = 8
LANES = 128
UNITS = 4
ROWS = 60
PAD = 64
GROUP = 4 * ROWS
WIDE = 4 * PAD


def spread(transposed):
    shape = (WIDE, GROUP) if transposed else (GROUP, WIDE)
    packed = lax.broadcasted_iota(jnp.int32, shape, 1 if transposed else 0)
    padded = lax.broadcasted_iota(jnp.int32, shape, 0 if transposed else 1)
    moved = packed + sum(jnp.where(packed >= k * ROWS, PAD - ROWS, 0) for k in (1, 2, 3))
    return jnp.where(moved == padded, 1.0, 0.0).astype(BF16)


def kernel(
    partners_hbm, mask_hbm, segs_hbm, master_hbm, hidden_hbm,
    hg_out, g_out,
    partners, mask, segs, master, hid, hid_t, hp, packing, growing, head, logits, sent, got_0, got_1, got_2, got_3, stage, other, scale, grad,
    dw, r1, s2, r2, s3, r3,
    local_sem, z_s, z_r, a_s, a_r, b_s, b_r, p1_s, p1_r, p2_s, p2_r,
    c_s, c_r, d_s, d_r, e_s, e_r,
):
    zl, co = lax.axis_index("zl"), lax.axis_index("co")
    zh, x, y = lax.axis_index("zh"), lax.axis_index("x"), lax.axis_index("y")
    me = zl * 2 + co
    tokens = hid.shape[0] // 2
    part = tokens // REPS
    got = (got_0, got_1, got_2, got_3)

    def rep_of(d):
        to = lax.rem(me + d, REPS)
        return to, {"zl": to // 2, "co": lax.rem(to, 2)}

    def first_of(q):
        return x * (1 - q) + y * q

    def second_of(q):
        return y * (1 - q) + x * q

    def on_first(q, d):
        return lax.rem(first_of(q) + d, 4), {"x": lax.rem(x + d * (1 - q), 4), "y": lax.rem(y + d * q, 4)}

    def on_second(q, d):
        return lax.rem(second_of(q) + d, 4), {"x": lax.rem(x + d * q, 4), "y": lax.rem(y + d * (1 - q), 4)}

    across = {"zh": 1 - zh}

    loads = [pltpu.make_async_copy(master_hbm, master, local_sem.at[0])]
    loads[0].start()

    barrier = pltpu.get_barrier_semaphore()
    peers = [across] + [rep_of(d)[1] for d in range(1, REPS)]
    peers += [side(0, d)[1] for side in (on_first, on_second) for d in (2, 1, 3)]
    for peer in peers:
        pl.semaphore_signal(barrier, inc=1, device_id=peer, device_id_type=MESH)

    others = ((hidden_hbm, hid), (mask_hbm, mask), (segs_hbm, segs), (partners_hbm, partners))
    for i, (src, dst) in enumerate(others, 1):
        copy = pltpu.make_async_copy(src, dst, local_sem.at[i])
        copy.start()
        loads.append(copy)

    loads[0].wait()
    low = master[:, 0, :].astype(BF16)
    vocab = low.shape[1]
    for u in range(UNITS):
        cols = min(LANES, vocab - u * LANES)
        piece = low[:, u * LANES : u * LANES + cols]
        if cols < LANES:
            piece = jnp.concatenate([piece, jnp.zeros((ROWS, LANES - cols), BF16)], axis=1)
        piece = jnp.concatenate([piece, jnp.zeros((PAD - ROWS, LANES), BF16)], axis=0)
        hp[u, zh, first_of(zh), second_of(zh)] = piece

    pl.semaphore_wait(barrier, len(peers))

    started = []

    def send(src, dst, send_sem, recv_sem, peer):
        copy = pltpu.make_async_remote_copy(
            src_ref=src, dst_ref=dst, send_sem=send_sem, recv_sem=recv_sem,
            device_id=peer, device_id_type=MESH,
        )
        copy.start()
        started.append(copy)
        return copy

    parts = ((0, 1), (1, UNITS))

    def leg_one(q, i):
        ref = hp.at[parts[i][0] : parts[i][1], q, first_of(q), second_of(q)]
        return [
            send(ref, ref, a_s.at[i, q, d - 1], a_r.at[i, q, d - 1], on_first(q, d)[1]) for d in (1, 2, 3)
        ]

    def leg_z(i):
        ref = hp.at[parts[i][0] : parts[i][1], zh, first_of(zh), second_of(zh)]
        return send(ref, ref, z_s.at[i], z_r.at[i], across)

    def leg_two(q, k):
        lo, hi = ((0, 1), (1, 2), (2, 4))[k]
        ref = hp.at[lo:hi, q, :, second_of(q)]
        return [
            send(ref, ref, b_s.at[q, k, d - 1], b_r.at[q, k, d - 1], on_second(q, d)[1]) for d in (1, 2, 3)
        ]

    def arrived(copies):
        for copy in copies:
            copy.wait_recv()

    def sent_all(count):
        for copy in started[:count]:
            copy.wait_send()
        del started[:count]

    near, far = zh, 1 - zh
    z_a = leg_z(0)
    near_a = leg_one(near, 0)
    z_b = leg_z(1)
    packing[...] = spread(False)
    arrived(near_a)
    near_0 = leg_two(near, 0)
    loads[1].wait()
    arrived([z_a])
    far_a = leg_one(far, 0)
    near_b = leg_one(near, 1)
    growing[...] = spread(True)
    arrived(far_a)
    far_0 = leg_two(far, 0)
    arrived([z_b])
    far_b = leg_one(far, 1)
    arrived(near_b)
    near_1 = leg_two(near, 1)

    def forward(u, between=None):
        lanes = slice(u * LANES, (u + 1) * LANES)
        for k in range(4):
            for q in range(2):
                block = hp[u, 0, k] if q == 0 else hp[u, 1, :, k]
                block = jnp.dot(packing[...], block.reshape(WIDE, LANES), preferred_element_type=F32)
                head[(4 * q + k) * GROUP : (4 * q + k + 1) * GROUP, lanes] = block.astype(BF16)

        @pl.loop(0, 2)
        def _(m):
            rows = pl.ds(pl.multiple_of(m * tokens, tokens), tokens)
            block = jnp.dot(hid[rows, :], head[:, lanes], preferred_element_type=F32)
            block = block.reshape(REPS, part, LANES)
            logits[u, :, m] = block
            sent[u, :, m] = block.astype(BF16)

        if between is not None:
            between()
        copies = []
        for d in range(1, REPS):
            to, peer = rep_of(d)
            copies.append(send(sent.at[u, to], got[u].at[me], p1_s.at[u, d - 1], p1_r.at[u, d - 1], peer))
        got[u][me] = sent[u, me]
        return copies

    def choose(u, copies):
        arrived(copies)
        after = []
        for d in range(1, REPS):
            to, peer = rep_of(d)
            for m in range(2):
                stage[u, d - 1, m] = got[u][partners[m, to], m]
            after.append(
                send(stage.at[u, d - 1], other.at[u, me], p2_s.at[u, d - 1], p2_r.at[u, d - 1], peer)
            )
        for m in range(2):
            other[u, me, m] = got[u][partners[m, me], m]
        return after

    def backward(u, copies, then=None):
        lanes = slice(u * LANES, (u + 1) * LANES)
        result = []
        arrived(copies)

        @pl.loop(0, REPS)
        def _(k):
            for m in range(2):
                rows = pl.ds(pl.multiple_of((m * REPS + k) * part, part), part)
                diff = logits[u, k, m] - other[u, k, m].astype(F32)
                grad[rows, lanes] = (diff * scale[rows, :]).astype(BF16)

        for q in range(2):
            for k in range(4):
                rows = slice((4 * q + k) * GROUP, (4 * q + k + 1) * GROUP)
                block = jnp.dot(hid_t[rows, :], grad[:, lanes], preferred_element_type=F32).astype(BF16)
                block = jnp.dot(growing[...], block, preferred_element_type=F32).astype(BF16)
                if q == 0:
                    dw[u, 0, k] = block.reshape(4, PAD, LANES)
                else:
                    dw[u, 1, :, k] = block.reshape(4, PAD, LANES)
            if then is not None:
                result.append(then(q))
        return result

    groups = ((0, 2), (2, 3), (3, 4))

    def reduce_one(i):
        lo, hi = groups[i]

        def half(q):
            copies = []
            for d in (1, 2, 3):
                to, peer = on_second(q, d)
                copies.append(
                    send(
                        dw.at[lo:hi, q, :, to], r1.at[q, d - 1, lo:hi],
                        c_s.at[i, q, d - 1], c_r.at[i, q, d - 1], peer,
                    )
                )
            return copies

        return half

    def reduce_two(i, before):
        lo, hi = groups[i]
        result = []
        for q in range(2):
            arrived(before[q])
            for u in range(lo, hi):
                for k in range(4):
                    total = dw[u, q, k, second_of(q)].astype(F32)
                    for d in range(3):
                        total = total + r1[q, d, u, k].astype(F32)
                    s2[u, q, k] = total.astype(BF16)
            copies = []
            for d in (1, 2, 3):
                to, peer = on_first(q, d)
                copies.append(
                    send(
                        s2.at[lo:hi, q, to], r2.at[q, d - 1, lo:hi],
                        d_s.at[i, q, d - 1], d_r.at[i, q, d - 1], peer,
                    )
                )
            result.append(copies)
        return result

    def reduce_three(i, before):
        lo, hi = groups[i]
        arrived(before[0] + before[1])

        def sum_half(q):
            for u in range(lo, hi):
                total = s2[u, q, first_of(q)].astype(F32)
                for d in range(3):
                    total = total + r2[q, d, u].astype(F32)
                s3[u, q] = total.astype(BF16)

        sum_half(1 - zh)
        copy = send(s3.at[lo:hi, 1 - zh], r3.at[lo:hi], e_s.at[i], e_r.at[i], across)
        sum_half(zh)
        return copy

    def finish(i, copy):
        lo, hi = groups[i]
        arrived([copy])
        for u in range(lo, hi):
            cols = min(LANES, vocab - u * LANES)
            total = s3[u, zh].astype(F32) + r3[u].astype(F32)
            g_out[:, 0, u * LANES : u * LANES + cols] = total[:ROWS, :cols]

    arrived(near_0 + far_0)
    far_1 = []

    def chunk_one():
        arrived(far_b)
        far_1.extend(leg_two(far, 1))

    p1_0 = forward(0, chunk_one)
    near_2 = leg_two(near, 2)
    for load in loads[2:]:
        load.wait()
    for m in range(2):
        valid = mask[m : m + 1, :].astype(F32)
        ids = segs[m : m + 1, :]
        onehot = (lax.broadcasted_iota(jnp.int32, (SEGS, tokens), 0) == ids).astype(F32)
        counts = jnp.sum(onehot * valid, axis=1, keepdims=True)
        per_frame = jnp.sum(onehot * counts, axis=0, keepdims=True)
        row = valid / jnp.maximum(per_frame, 1.0)
        scale[m * tokens : (m + 1) * tokens, :] = jnp.broadcast_to(row, (LANES, tokens)).T
    arrived(near_1 + far_1)
    far_2 = leg_two(far, 2)
    p1_1 = forward(1)
    p2_0 = choose(0, p1_0)
    arrived(near_2 + far_2)
    p1_2 = forward(2)

    @pl.loop(0, hid_t.shape[0] // LANES)
    def _(j):
        at = pl.ds(pl.multiple_of(j * LANES, LANES), LANES)
        hid_t[at, :] = hid[:, at].T

    p2_1 = choose(1, p1_1)
    p1_3 = forward(3)
    early = len(started)
    backward(0, p2_0)
    p2_2 = choose(2, p1_2)
    c_0 = backward(1, p2_1, reduce_one(0))
    p2_3 = choose(3, p1_3)
    sent_all(early)
    d_0 = reduce_two(0, c_0)
    c_1 = backward(2, p2_2, reduce_one(1))
    e_0 = reduce_three(0, d_0)
    c_2 = backward(3, p2_3, reduce_one(2))
    d_1 = reduce_two(1, c_1)

    def hidden_gradient(t):
        rows = slice(t * WIDE, (t + 1) * WIDE)
        width = 3 * LANES

        @pl.loop(0, hid.shape[1] // width)
        def _(n):
            at = pl.ds(pl.multiple_of(n * width, LANES), width)
            block = lax.dot_general(
                grad[rows, :], head[at, :], (((1,), (1,)), ((), ())), preferred_element_type=F32
            )
            hg_out[rows, at] = block.astype(BF16)

    hidden_gradient(0)
    hidden_gradient(1)
    hidden_gradient(2)
    d_2 = reduce_two(2, c_2)
    e_1 = reduce_three(1, d_1)
    hidden_gradient(3)
    e_2 = reduce_three(2, d_2)
    finish(0, e_0)
    finish(1, e_1)
    sent_all(len(started))
    finish(2, e_2)


def adam(hg, head_grad, master, moment_one, moment_two, hg_out, new_master, new_m1, new_m2, held, sems):
    height = hg.shape[0] // 4
    for t in range(4):
        rows = pl.ds(t * height, height)
        pltpu.make_async_copy(hg.at[rows], hg_out.at[rows], sems.at[7 + t]).start()
    loads = [
        pltpu.make_async_copy(ref, held.at[i], sems.at[i])
        for i, ref in enumerate((head_grad, master, moment_one, moment_two))
    ]
    for load in loads:
        load.start()
    for load in loads:
        load.wait()
    g = held[0]
    one = 0.9 * held[2] + 0.1 * g
    two = 0.99 * held[3] + 0.01 * g * g
    held[5] = one
    held[6] = two
    held[4] = held[1] - 0.01 * one / (jnp.sqrt(two) + 1e-08)
    stores = [
        pltpu.make_async_copy(held.at[4 + i], ref, sems.at[4 + i])
        for i, ref in enumerate((new_master, new_m1, new_m2))
    ]
    for store in stores:
        store.start()
    for store in stores:
        store.wait()
    for t in range(4):
        rows = pl.ds(t * height, height)
        pltpu.make_async_copy(hg.at[rows], hg_out.at[rows], sems.at[7 + t]).wait()


def per_device(hidden, partners, frame_mask, segment_ids, master, moment_one, moment_two):
    tokens, depth = hidden.shape[2:]
    frames = 2 * tokens
    part = tokens // REPS
    wide = UNITS * LANES
    vocab = master.shape[2]
    vmem = pl.BlockSpec(memory_space=pltpu.VMEM)
    hbm = pl.BlockSpec(memory_space=pl.ANY)
    dma = pltpu.SemaphoreType.DMA
    exchange = (REPS, 2, part, LANES)
    hg, head_grad = pl.pallas_call(
        kernel,
        out_shape=(pltpu.VMEM((frames, depth), BF16), pltpu.VMEM((ROWS, 1, vocab), F32)),
        in_specs=[pl.BlockSpec(memory_space=pl.ANY)] * 5,
        out_specs=(vmem, vmem),
        scratch_shapes=[
            pltpu.SMEM((2, REPS), jnp.int32),
            pltpu.VMEM((2, tokens), jnp.int32),
            pltpu.VMEM((2, tokens), jnp.int32),
            pltpu.VMEM((ROWS, 1, vocab), F32),
            pltpu.VMEM((frames, depth), BF16),
            pltpu.VMEM((depth, frames), BF16),
            pltpu.VMEM((UNITS, 2, 4, 4, PAD, LANES), BF16),
            pltpu.VMEM((GROUP, WIDE), BF16),
            pltpu.VMEM((WIDE, GROUP), BF16),
            pltpu.VMEM((depth, wide), BF16),
            pltpu.VMEM((UNITS, *exchange), F32),
            pltpu.VMEM((UNITS, *exchange), BF16),
            pltpu.VMEM(exchange, BF16),
            pltpu.VMEM(exchange, BF16),
            pltpu.VMEM(exchange, BF16),
            pltpu.VMEM(exchange, BF16),
            pltpu.VMEM((UNITS, REPS - 1, 2, part, LANES), BF16),
            pltpu.VMEM((UNITS, *exchange), BF16),
            pltpu.VMEM((frames, LANES), F32),
            pltpu.VMEM((frames, wide), BF16),
            pltpu.VMEM((UNITS, 2, 4, 4, PAD, LANES), BF16),
            pltpu.VMEM((2, 3, UNITS, 4, PAD, LANES), BF16),
            pltpu.VMEM((UNITS, 2, 4, PAD, LANES), BF16),
            pltpu.VMEM((2, 3, UNITS, PAD, LANES), BF16),
            pltpu.VMEM((UNITS, 2, PAD, LANES), BF16),
            pltpu.VMEM((UNITS, PAD, LANES), BF16),
            dma((5,)),
            dma((2,)), dma((2,)),
            dma((2, 2, 3)), dma((2, 2, 3)),
            dma((2, 3, 3)), dma((2, 3, 3)),
            dma((UNITS, 7)), dma((UNITS, 7)),
            dma((UNITS, 7)), dma((UNITS, 7)),
            dma((3, 2, 3)), dma((3, 2, 3)),
            dma((3, 2, 3)), dma((3, 2, 3)),
            dma((3,)), dma((3,)),
        ],
        compiler_params=pltpu.CompilerParams(
            collective_id=0, has_side_effects=True, vmem_limit_bytes=52 << 20
        ),
        name="codistill",
    )(
        partners, frame_mask, segment_ids, master.reshape(ROWS, 1, vocab), hidden.reshape(frames, depth),
    )
    flat = (ROWS, 1, vocab)
    small = jax.ShapeDtypeStruct(flat, F32)
    hg, new_master, new_m1, new_m2 = pl.pallas_call(
        adam,
        out_shape=(jax.ShapeDtypeStruct(hg.shape, BF16), small, small, small),
        in_specs=[hbm] * 5,
        out_specs=(hbm,) * 4,
        scratch_shapes=[pltpu.VMEM((7, *flat), F32), dma((11,))],
        compiler_params=pltpu.CompilerParams(vmem_limit_bytes=8 << 20),
        name="adam",
    )(hg, head_grad, master.reshape(flat), moment_one.reshape(flat), moment_two.reshape(flat))
    shape = master.shape
    return hg.reshape(hidden.shape), new_master.reshape(shape), new_m1.reshape(shape), new_m2.reshape(shape)


def solution(mesh):
    axes = ("zl", "co", "zh", "x", "y")
    torus = Mesh(mesh.devices.reshape(4, 2, 2, 4, 4), axes)
    rep, dp = ("zl", "co"), ("zh", "x", "y")
    in_specs = (
        P(None, rep, dp, None),
        P(),
        P(None, dp),
        P(None, dp),
        P(rep, dp, None),
        P(rep, dp, None),
        P(rep, dp, None),
    )
    out_specs = (
        P(None, rep, dp, None),
        P(rep, dp, None),
        P(rep, dp, None),
        P(rep, dp, None),
    )
    return jax.shard_map(
        per_device, mesh=torus, in_specs=in_specs, out_specs=out_specs, check_vma=False
    )
```
